32 devices in a mesh: fsdp: 2 (over y), context: 4 (over z), tensor: 4 (over x, core).
Axes of the slice: x: 2, y: 2, z: 4, core: 2. Of those that a mesh axis runs over, the one named last changes fastest.
Arguments:
- frames: bfloat16 [1536, 4, 1536], P(('context', 'tensor'), 'fsdp'), may hold values from -6 to 6
- text_states: bfloat16 [64, 4, 1536], P(None, 'fsdp'), may hold values from -6 to 6
- cotangent: bfloat16 [1536, 4, 1536], P(('context', 'tensor'), 'fsdp'), may hold values from -6 to 6
- self_query: bfloat16 [1536, 1536], P(('fsdp', 'context'), 'tensor'), may hold values from -0.15625 to 0.15625
- self_key: bfloat16 [1536, 1536], P(('fsdp', 'context'), 'tensor'), may hold values from -0.15625 to 0.15625
- self_value: bfloat16 [1536, 1536], P(('fsdp', 'context'), 'tensor'), may hold values from -0.15625 to 0.15625
- self_out: bfloat16 [1536, 1536], P(('fsdp', 'context'), 'tensor'), may hold values from -1.25 to 1.25
- cross_query: bfloat16 [1536, 1536], P(('fsdp', 'context'), 'tensor'), may hold values from -0.15625 to 0.15625
- cross_key: bfloat16 [1536, 1536], P(('fsdp', 'context'), 'tensor'), may hold values from -0.15625 to 0.15625
- cross_value: bfloat16 [1536, 1536], P(('fsdp', 'context'), 'tensor'), may hold values from -0.15625 to 0.15625
- cross_out: bfloat16 [1536, 1536], P(('fsdp', 'context'), 'tensor'), may hold values from -0.875 to 0.875
- feed_in: bfloat16 [1536, 6144], P(('fsdp', 'context'), 'tensor'), may hold values from -0.15625 to 0.15625
- feed_out: bfloat16 [1536, 6144], P(('fsdp', 'context'), 'tensor'), may hold values from -0.078125 to 0.078125
- first_gain: bfloat16 [1536], P(('fsdp', 'context')), may hold values from 0.25 to 1.75
- first_shift: bfloat16 [1536], P(('fsdp', 'context')), may hold values from -3 to 3
- second_gain: bfloat16 [1536], P(('fsdp', 'context')), may hold values from 0.25 to 1.75
- second_shift: bfloat16 [1536], P(('fsdp', 'context')), may hold values from -3 to 3
- third_gain: bfloat16 [1536], P(('fsdp', 'context')), may hold values from 0.25 to 1.75
- third_shift: bfloat16 [1536], P(('fsdp', 'context')), may hold values from -3 to 3
Outputs:
- layer_out: bfloat16 [1536, 4, 1536], P(('context', 'tensor'), 'fsdp')
- frames_grad: float32 [1536, 4, 1536], P(('context', 'tensor'), 'fsdp')
- text_grad: float32 [64, 4, 1536], P(None, 'fsdp')
- self_query_grad: float32 [1536, 1536], P(('fsdp', 'context'), 'tensor')
- self_key_grad: float32 [1536, 1536], P(('fsdp', 'context'), 'tensor')
- self_value_grad: float32 [1536, 1536], P(('fsdp', 'context'), 'tensor')
- self_out_grad: float32 [1536, 1536], P(('fsdp', 'context'), 'tensor')
- cross_query_grad: float32 [1536, 1536], P(('fsdp', 'context'), 'tensor')
- cross_key_grad: float32 [1536, 1536], P(('fsdp', 'context'), 'tensor')
- cross_value_grad: float32 [1536, 1536], P(('fsdp', 'context'), 'tensor')
- cross_out_grad: float32 [1536, 1536], P(('fsdp', 'context'), 'tensor')
- feed_in_grad: float32 [1536, 6144], P(('fsdp', 'context'), 'tensor')
- feed_out_grad: float32 [1536, 6144], P(('fsdp', 'context'), 'tensor')
- first_gain_grad: float32 [1536], P(('fsdp', 'context'))
- first_shift_grad: float32 [1536], P(('fsdp', 'context'))
- second_gain_grad: float32 [1536], P(('fsdp', 'context'))
- second_shift_grad: float32 [1536], P(('fsdp', 'context'))
- third_gain_grad: float32 [1536], P(('fsdp', 'context'))
- third_shift_grad: float32 [1536], P(('fsdp', 'context'))
The draws below stay inside these ranges and needn't reach their ends.
All inputs are finite; a program needn't handle non-finite values.
Results may differ from the reference program's by a relative error of at most 0.015.
Values may be sent and summed in bfloat16 or wider, within the bound.
No kernel may reach another device: no remote copies, remote signals or barrier semaphores. Data moves between devices by JAX's collectives and lax.ppermute only.
A program may use at most 192 MiB of HBM per device.

```python
import jax
import jax.numpy as jnp
from jax import lax

D = 1536
HEAD = 64
FF = 6144
TEXT = 64
CLIPS = 4
FRAMES = 1536


def steps_of(rng, dims, split, smallest, largest):
    level = 1.0
    for dim, blocks in split:
        steps = jax.random.uniform(jax.random.fold_in(jax.random.fold_in(rng, 6), dim), (blocks,), jnp.float32, smallest / len(split), largest / len(split))
        level = level * jnp.repeat(jnp.exp(steps), dims[dim] // blocks).reshape((-1,) + (1,) * (len(dims) - 1 - dim))
    return level


def scatter_about(key, shape, scale, reach, shards=(), held_as=jnp.bfloat16):
    entries = scale * jax.random.normal(key, shape, jnp.float32)
    if shards:
        entries = entries * steps_of(key, shape, shards, -0.22, 0.18)
    return jnp.clip(entries, -reach, reach).astype(held_as)


def setup_inputs(seed: int = 0) -> dict:
    arg_keys = jax.random.split(jax.random.key(seed), 20)
    frames = scatter_about(arg_keys[0], (FRAMES, CLIPS, D), 1.0, 6.0, ((0, 16), (1, 2)))
    text_states = scatter_about(arg_keys[1], (TEXT, CLIPS, D), 1.0, 6.0, ((1, 2),))
    cotangent = scatter_about(arg_keys[2], (FRAMES, CLIPS, D), 1.0, 6.0, ((0, 16), (1, 2)))
    self_query = scatter_about(arg_keys[3], (D, D), D ** -0.5, 0.15625, ((0, 8), (1, 4)))
    self_key = scatter_about(arg_keys[4], (D, D), D ** -0.5, 0.15625, ((0, 8), (1, 4)))
    self_value = scatter_about(arg_keys[5], (D, D), D ** -0.5, 0.15625, ((0, 8), (1, 4)))
    self_out = scatter_about(arg_keys[6], (D, D), (D // 64) ** -0.5, 1.25, ((0, 8), (1, 4)))
    cross_query = scatter_about(arg_keys[7], (D, D), D ** -0.5, 0.15625, ((0, 8), (1, 4)))
    cross_key = scatter_about(arg_keys[8], (D, D), D ** -0.5, 0.15625, ((0, 8), (1, 4)))
    cross_value = scatter_about(arg_keys[9], (D, D), D ** -0.5, 0.15625, ((0, 8), (1, 4)))
    cross_out = scatter_about(arg_keys[10], (D, D), (D // 32) ** -0.5, 0.875, ((0, 8), (1, 4)))
    feed_in = scatter_about(arg_keys[11], (D, FF), D ** -0.5, 0.15625, ((0, 8), (1, 4)))
    feed_out = scatter_about(arg_keys[12], (D, FF), FF ** -0.5, 0.078125, ((0, 8), (1, 4)))
    first_gain = jnp.clip(1.0 + 0.15 * jax.random.normal(arg_keys[13], (D,), jnp.float32), 0.25, 1.75).astype(jnp.bfloat16)
    first_shift = scatter_about(arg_keys[14], (D,), 0.5, 3.0, ((0, 8),))
    second_gain = jnp.clip(1.0 + 0.15 * jax.random.normal(arg_keys[15], (D,), jnp.float32), 0.25, 1.75).astype(jnp.bfloat16)
    second_shift = scatter_about(arg_keys[16], (D,), 0.5, 3.0, ((0, 8),))
    third_gain = jnp.clip(1.0 + 0.15 * jax.random.normal(arg_keys[17], (D,), jnp.float32), 0.25, 1.75).astype(jnp.bfloat16)
    third_shift = scatter_about(arg_keys[18], (D,), 0.5, 3.0, ((0, 8),))
    return dict(frames=frames, text_states=text_states, cotangent=cotangent, self_query=self_query, self_key=self_key, self_value=self_value, self_out=self_out, cross_query=cross_query, cross_key=cross_key, cross_value=cross_value, cross_out=cross_out, feed_in=feed_in, feed_out=feed_out, first_gain=first_gain, first_shift=first_shift, second_gain=second_gain, second_shift=second_shift, third_gain=third_gain, third_shift=third_shift)


highest = lax.Precision.HIGHEST
masked_score = -1e+30

@jax.custom_vjp
def low(v):
    return lax.optimization_barrier(v.astype(jnp.bfloat16)).astype(jnp.float32)

@jax.custom_vjp
def low_back(v):
    return v

def low_keep(v):
    return (low(v), None)

def low_pass(kept, grad):
    return (grad,)

def back_keep(v):
    return (v, None)

def back_low(kept, grad):
    return (low(grad),)
low.defvjp(low_keep, low_pass)
low_back.defvjp(back_keep, back_low)

def layer_norm(values, gain, shift):
    centre = lax.optimization_barrier(jnp.mean(values, axis=-1, keepdims=True))
    centred = values - centre
    spread = lax.optimization_barrier(jnp.mean(centred * centred, axis=-1, keepdims=True))
    return centred * lax.rsqrt(spread + 1e-05) * gain + shift

def project_in(rows, weight):
    return jnp.einsum('fcd,de->fce', rows, weight, precision=highest)

def project_out(rows, weight):
    return jnp.einsum('fce,de->fcd', rows, weight, precision=highest)

def split_heads(values):
    frame_count, clip_count, feature_width = values.shape
    head_count = feature_width // HEAD
    arranged = values.reshape(frame_count, clip_count, head_count, HEAD).transpose(1, 2, 0, 3)
    return arranged.reshape(clip_count * head_count, frame_count, HEAD)

def merge_heads(values, clip_count):
    groups, frame_count, head_size = values.shape
    head_count = groups // clip_count
    arranged = values.reshape(clip_count, head_count, frame_count, head_size).transpose(2, 0, 1, 3)
    return arranged.reshape(frame_count, clip_count, head_count * head_size)

def causal_head(operands):
    queries, key_rows, value_rows = operands
    frame_count = queries.shape[0]
    scores = low_back(jnp.dot(queries, key_rows.T, precision=highest) * queries.shape[-1] ** (-0.5))
    allowed = lax.broadcasted_iota(jnp.int32, (frame_count, frame_count), 1) <= lax.broadcasted_iota(jnp.int32, (frame_count, frame_count), 0)
    weights = low(jax.nn.softmax(jnp.where(allowed, scores, masked_score), axis=-1))
    return jnp.dot(weights, value_rows, precision=highest)

def cross_head(operands):
    queries, key_rows, value_rows = operands
    scores = low_back(jnp.dot(queries, key_rows.T, precision=highest) * queries.shape[-1] ** (-0.5))
    weights = low(jax.nn.softmax(scores, axis=-1))
    return jnp.dot(weights, value_rows, precision=highest)

def layer_forward(frames, text_states, self_query, self_key, self_value, self_out, cross_query, cross_key, cross_value, cross_out, feed_in, feed_out, first_gain, first_shift, second_gain, second_shift, third_gain, third_shift):
    clip_count = frames.shape[1]
    normed_one = low(layer_norm(frames, first_gain, first_shift))
    queries = low(low_back(project_in(normed_one, self_query)))
    key_rows = low(low_back(project_in(normed_one, self_key)))
    value_rows = low(low_back(project_in(normed_one, self_value)))
    attended = lax.map(jax.checkpoint(causal_head), (split_heads(queries), split_heads(key_rows), split_heads(value_rows)))
    attended = low(low_back(merge_heads(attended, clip_count)))
    after_self = frames + low_back(project_out(attended, self_out))
    normed_two = low(layer_norm(after_self, second_gain, second_shift))
    cross_queries = low(low_back(project_in(normed_two, cross_query)))
    cross_keys = low(project_in(text_states, cross_key))
    cross_values = low(project_in(text_states, cross_value))
    crossed = lax.map(jax.checkpoint(cross_head), (split_heads(cross_queries), split_heads(cross_keys), split_heads(cross_values)))
    crossed = low(low_back(merge_heads(crossed, clip_count)))
    after_cross = after_self + low_back(project_out(crossed, cross_out))
    normed_three = low(layer_norm(after_cross, third_gain, third_shift))
    hidden = low_back(project_in(normed_three, feed_in))
    active = low(jax.nn.gelu(hidden, approximate=False))
    return after_cross + low_back(project_out(active, feed_out))

def reference(frames, text_states, cotangent, self_query, self_key, self_value, self_out, cross_query, cross_key, cross_value, cross_out, feed_in, feed_out, first_gain, first_shift, second_gain, second_shift, third_gain, third_shift):
    inputs = [item.astype(jnp.float32) for item in (frames, text_states, self_query, self_key, self_value, self_out, cross_query, cross_key, cross_value, cross_out, feed_in, feed_out, first_gain, first_shift, second_gain, second_shift, third_gain, third_shift)]
    output, pullback = jax.vjp(layer_forward, *inputs)
    grads = pullback(cotangent.astype(jnp.float32))
    return (output.astype(jnp.bfloat16), grads[0], grads[1], grads[2], grads[3], grads[4], grads[5], grads[6], grads[7], grads[8], grads[9], grads[10], grads[11], grads[12], grads[13], grads[14], grads[15], grads[16], grads[17])
```

```python
import functools

import jax
import jax.numpy as jnp
from jax import lax
from jax.experimental import pallas as pl
from jax.experimental.pallas import tpu as pltpu
from jax.sharding import PartitionSpec as P

HEAD = 64
low = jnp.bfloat16
wide = jnp.float32
masked_score = -1e30
scale = HEAD**-0.5


def dot(left, right, left_dim, right_dim):
    return lax.dot_general(
        left, right, (((left_dim,), (right_dim,)), ((), ())), preferred_element_type=wide
    )


def from_context(values, step, size):
    return lax.ppermute(values, "context", [((i + step) % size, i) for i in range(size)])


def from_fsdp(values, step, size):
    return lax.ppermute(values, "fsdp", [((i + step) % size, i) for i in range(size)])


def swap_tensor(values, mask, size):
    return lax.ppermute(values, "tensor", [(i, i ^ mask) for i in range(size)])


def shift_order(size):
    order = []
    for step in range(1, size // 2 + 1):
        order.append(step)
        if size - step != step:
            order.append(size - step)
    return order


def gather_group(shard, fsdp_size, context_size, axis=0):
    arrived = {0: shard}
    for step in shift_order(context_size):
        arrived[step] = from_context(shard, step, context_size)
    pieces = [arrived[step] for step in range(context_size)]
    for far in range(1, fsdp_size):
        there = {0: from_fsdp(shard, far, fsdp_size)}
        for step in shift_order(context_size):
            there[step] = from_fsdp(arrived[step], far, fsdp_size)
        pieces += [there[step] for step in range(context_size)]
    return jnp.concatenate(pieces, axis=axis)


def reduce_fsdp(near, far_blocks, fsdp_size):
    total = near
    for step in range(1, fsdp_size):
        total = total + from_fsdp(far_blocks[step - 1], fsdp_size - step, fsdp_size).astype(wide)
    return total


def reduce_context(total, context_size):
    rows = total.shape[0] // context_size
    result = total[:rows]
    for step in shift_order(context_size):
        piece = total[step * rows : (step + 1) * rows].astype(low)
        result = result + from_context(piece, context_size - step, context_size).astype(wide)
    return result


def weight_grad(left_rows, right_rows, fsdp_size, context_size):
    half = left_rows.shape[-1] // fsdp_size
    far = [
        dot(left_rows[:, step * half : (step + 1) * half], right_rows, 0, 0).astype(low)
        for step in range(1, fsdp_size)
    ]
    near = dot(left_rows[:, :half], right_rows, 0, 0)
    return reduce_context(reduce_fsdp(near, far, fsdp_size), context_size)


def gather_rows(values, tensor_size):
    blocks = [values]
    mask = tensor_size // 2
    while mask:
        blocks = blocks + [swap_tensor(block, mask, tensor_size) for block in blocks]
        mask //= 2
    return jnp.concatenate(blocks, axis=1)


def mask_order(tensor_size):
    order = [0]
    mask = tensor_size // 2
    while mask:
        order = order + [item ^ mask for item in order]
        mask //= 2
    return order


def scatter_rows(parts, tensor_size):
    mask = 1
    while mask < tensor_size:
        half = parts.shape[1] // 2
        arrived = swap_tensor(parts[:, half:].astype(low), mask, tensor_size)
        parts = parts[:, :half] + arrived.astype(wide)
        mask *= 2
    return parts


def norm_stats(values):
    centre = jnp.mean(values, axis=-1, keepdims=True)
    centred = values - centre
    spread = jnp.mean(centred * centred, axis=-1, keepdims=True)
    root = lax.rsqrt(spread + 1e-05)
    return centred * root, root


def layer_norm(values, gain, shift):
    scaled, unused = norm_stats(values)
    return (scaled * gain + shift).astype(low)


def norm_back(values, gain, grad):
    scaled, root = norm_stats(values)
    weighted = grad * gain
    inner = jnp.mean(weighted * scaled, axis=-1, keepdims=True)
    outer = jnp.mean(weighted, axis=-1, keepdims=True)
    piece = root * (weighted - outer - scaled * inner)
    return piece, jnp.sum(grad * scaled, axis=(0, 1)), jnp.sum(grad, axis=(0, 1))


def frame_places(shape, axis, frames, order, own):
    row = lax.broadcasted_iota(jnp.int32, shape, axis)
    place = jnp.zeros(shape, jnp.int32)
    for slot, mask in enumerate(order):
        inside = (row >= slot * frames) & (row < (slot + 1) * frames)
        place = jnp.where(inside, (own ^ mask) * frames + row - slot * frames, place)
    return place


def fill_bias(bias_ref, frames, order, own):
    shape = bias_ref.shape
    keys = frame_places(shape, 0, frames, order, own)
    queries = frame_places(shape, 1, frames, order, own)
    bias_ref[...] = jnp.where(keys <= queries, 0.0, masked_score).astype(wide)


def self_forward_kernel(frames, order, place_ref, rows_ref, out_ref, top_ref, bias_ref):
    blocks, block_rows = rows_ref.shape[0], rows_ref.shape[1]
    width = out_ref.shape[2]
    heads = width // HEAD
    own_block = place_ref[0]
    fill_bias(bias_ref, frames, order, place_ref[1])

    def slot_of(block):
        return lax.rem(own_block - block + blocks, blocks)

    def query_block(block, unused):
        slot = slot_of(block)
        outs = []
        for head in range(heads):
            lanes = head * HEAD
            query = rows_ref[slot, :, lanes : lanes + HEAD] * scale

            def key_value(where, lanes=lanes):
                key = rows_ref[where, :, width + lanes : width + lanes + HEAD]
                value = rows_ref[where, :, 2 * width + lanes : 2 * width + lanes + HEAD]
                return key, value

            key, value = key_value(slot)
            scores = dot(key, query, 1, 1) + bias_ref[...]
            top = jnp.max(scores, axis=0, keepdims=True)
            weights = jnp.exp(scores - top)
            total = jnp.sum(weights, axis=0, keepdims=True)
            acc = dot(value, weights.astype(low), 0, 0)

            def step(past, carry, query=query, key_value=key_value):
                top, total, acc = carry
                key, value = key_value(slot_of(past))
                scores = dot(key, query, 1, 1)
                new_top = jnp.maximum(top, jnp.max(scores, axis=0, keepdims=True))
                weights = jnp.exp(scores - new_top)
                shrink = jnp.exp(top - new_top)
                total = total * shrink + jnp.sum(weights, axis=0, keepdims=True)
                acc = acc * shrink + dot(value, weights.astype(low), 0, 0)
                return new_top, total, acc

            top, total, acc = lax.fori_loop(0, block, step, (top, total, acc))
            outs.append((acc / total).T)
            top_ref[slot, head : head + 1, :] = top + jnp.log(total)
        out_ref[slot] = jnp.concatenate(outs, axis=1).astype(low)
        return unused

    lax.fori_loop(0, blocks, query_block, 0)


def self_backward_kernel(
    frames,
    order,
    place_ref,
    rows_ref,
    out_ref,
    top_ref,
    grad_ref,
    result_ref,
    bias_ref,
    delta_ref,
    query_acc,
    key_acc,
    value_acc,
):
    blocks, block_rows = rows_ref.shape[0], rows_ref.shape[1]
    width = out_ref.shape[2]
    heads = width // HEAD
    own_block = place_ref[0]
    fill_bias(bias_ref, frames, order, place_ref[1])
    query_acc[...] = jnp.zeros_like(query_acc)

    def slot_of(block):
        return lax.rem(own_block - block + blocks, blocks)

    def fill_delta(slot, unused):
        for head in range(heads):
            lanes = head * HEAD
            product = out_ref[slot, :, lanes : lanes + HEAD].astype(wide) * grad_ref[
                slot, :, lanes : lanes + HEAD
            ].astype(wide)
            delta_ref[slot, head : head + 1, :] = jnp.sum(product.T, axis=0, keepdims=True)
        return unused

    lax.fori_loop(0, blocks, fill_delta, 0)

    def key_block(block, unused):
        slot = slot_of(block)
        for head in range(heads):
            lanes = head * HEAD
            key = rows_ref[slot, :, width + lanes : width + lanes + HEAD]
            value = rows_ref[slot, :, 2 * width + lanes : 2 * width + lanes + HEAD]

            def terms(where, bias, lanes=lanes, head=head, key=key, value=value):
                query = rows_ref[where, :, lanes : lanes + HEAD] * scale
                grad = grad_ref[where, :, lanes : lanes + HEAD]
                scores = dot(key, query, 1, 1)
                if bias is not None:
                    scores = scores + bias
                weights = jnp.exp(scores - top_ref[where, head : head + 1, :])
                grad_weights = dot(value, grad, 1, 1)
                grad_scores = (weights * (grad_weights - delta_ref[where, head : head + 1, :])).astype(low)
                query_acc[head, where] += dot(key, grad_scores, 0, 0)
                return dot(grad_scores, query, 1, 0), dot(weights.astype(low), grad, 1, 0)

            start = terms(slot, bias_ref[...])

            def step(later, carry, terms=terms):
                key_part, value_part = terms(slot_of(later), None)
                return carry[0] + key_part, carry[1] + value_part

            key_grad, value_grad = lax.fori_loop(block + 1, blocks, step, start)
            key_acc[head, slot] = key_grad
            value_acc[head, slot] = value_grad
        return unused

    lax.fori_loop(0, blocks, key_block, 0)

    def write(slot, unused):
        parts = [(query_acc[head, slot] * scale).T for head in range(heads)]
        parts += [key_acc[head, slot] for head in range(heads)]
        parts += [value_acc[head, slot] for head in range(heads)]
        rest = result_ref.shape[2] - 3 * width
        if rest:
            parts.append(jnp.zeros((block_rows, rest), wide))
        result_ref[slot] = jnp.concatenate(parts, axis=1).astype(low)
        return unused

    lax.fori_loop(0, blocks, write, 0)


smem = pl.BlockSpec(memory_space=pltpu.SMEM)
vmem = pl.BlockSpec(memory_space=pltpu.VMEM)
kernel_params = pltpu.CompilerParams(vmem_limit_bytes=40 * 1024 * 1024)


def self_forward(place, rows, width, frames, order):
    blocks, block_rows, unused = rows.shape
    heads = width // HEAD
    work = blocks * block_rows * blocks * block_rows * heads * 5 // 8
    return pl.pallas_call(
        functools.partial(self_forward_kernel, frames, order),
        out_shape=(
            jax.ShapeDtypeStruct((blocks, block_rows, width), low),
            jax.ShapeDtypeStruct((blocks, heads, block_rows), wide),
        ),
        in_specs=[smem, vmem],
        out_specs=(vmem, vmem),
        scratch_shapes=[pltpu.VMEM((block_rows, block_rows), wide)],
        compiler_params=kernel_params,
        cost_estimate=pl.CostEstimate(
            flops=work * 64 * 4, bytes_accessed=rows.size * 4, transcendentals=work
        ),
    )(place, rows)


def self_backward(place, rows, out, top, grad, frames, order):
    blocks, block_rows, full = rows.shape
    width = out.shape[2]
    heads = width // HEAD
    work = blocks * block_rows * blocks * block_rows * heads * 5 // 8
    return pl.pallas_call(
        functools.partial(self_backward_kernel, frames, order),
        out_shape=jax.ShapeDtypeStruct((blocks, block_rows, full), low),
        in_specs=[smem, vmem, vmem, vmem, vmem],
        out_specs=vmem,
        scratch_shapes=[
            pltpu.VMEM((block_rows, block_rows), wide),
            pltpu.VMEM((blocks, heads, block_rows), wide),
            pltpu.VMEM((heads, blocks, HEAD, block_rows), wide),
            pltpu.VMEM((heads, blocks, block_rows, HEAD), wide),
            pltpu.VMEM((heads, blocks, block_rows, HEAD), wide),
        ],
        compiler_params=kernel_params,
        cost_estimate=pl.CostEstimate(
            flops=work * 64 * 10, bytes_accessed=rows.size * 8, transcendentals=work
        ),
    )(place, rows, out, top, grad)


def cross_weights(query, key):
    scores = dot(key, query * scale, 1, 1)
    top = jnp.max(scores, axis=0, keepdims=True)
    weights = jnp.exp(scores - top)
    return weights / jnp.sum(weights, axis=0, keepdims=True)


def cross_forward_kernel(query_ref, key_ref, value_ref, out_ref):
    outs = []
    for head in range(query_ref.shape[2] // HEAD):
        lanes = slice(head * HEAD, (head + 1) * HEAD)
        weights = cross_weights(query_ref[0, :, lanes], key_ref[0, :, lanes])
        outs.append(dot(value_ref[0, :, lanes], weights.astype(low), 0, 0).T)
    out_ref[0] = jnp.concatenate(outs, axis=1).astype(low)


def cross_backward_kernel(query_ref, key_ref, value_ref, grad_ref, query_out, key_out, value_out):
    queries, keys, values = [], [], []
    for head in range(query_ref.shape[2] // HEAD):
        lanes = slice(head * HEAD, (head + 1) * HEAD)
        query, key, value = query_ref[0, :, lanes], key_ref[0, :, lanes], value_ref[0, :, lanes]
        grad = grad_ref[0, :, lanes]
        weights = cross_weights(query, key)
        grad_weights = dot(value, grad, 1, 1)
        inner = jnp.sum(weights * grad_weights, axis=0, keepdims=True)
        grad_scores = (weights * (grad_weights - inner)).astype(low)
        queries.append((dot(key, grad_scores, 0, 0) * scale).T)
        keys.append(dot(grad_scores, query * scale, 1, 0))
        values.append(dot(weights.astype(low), grad, 1, 0))
    query_out[0] = jnp.concatenate(queries, axis=1).astype(low)
    key_out[0] = jnp.concatenate(keys, axis=1)
    value_out[0] = jnp.concatenate(values, axis=1)


def clip_spec(shape):
    return pl.BlockSpec((1,) + tuple(shape[1:]), lambda clip: (clip, 0, 0))


def cross_forward(query, key, value):
    work = query.shape[0] * query.shape[1] * query.shape[2] * key.shape[1]
    return pl.pallas_call(
        cross_forward_kernel,
        grid=(query.shape[0],),
        out_shape=jax.ShapeDtypeStruct(query.shape, low),
        in_specs=[clip_spec(query.shape), clip_spec(key.shape), clip_spec(value.shape)],
        out_specs=clip_spec(query.shape),
        compiler_params=kernel_params,
        cost_estimate=pl.CostEstimate(
            flops=4 * work, bytes_accessed=4 * query.size, transcendentals=work // 64
        ),
    )(query, key, value)


def cross_backward(query, key, value, grad):
    work = query.shape[0] * query.shape[1] * query.shape[2] * key.shape[1]
    return pl.pallas_call(
        cross_backward_kernel,
        grid=(query.shape[0],),
        out_shape=(
            jax.ShapeDtypeStruct(query.shape, low),
            jax.ShapeDtypeStruct(key.shape, wide),
            jax.ShapeDtypeStruct(value.shape, wide),
        ),
        in_specs=[
            clip_spec(query.shape),
            clip_spec(key.shape),
            clip_spec(value.shape),
            clip_spec(grad.shape),
        ],
        out_specs=(clip_spec(query.shape), clip_spec(key.shape), clip_spec(value.shape)),
        compiler_params=kernel_params,
        cost_estimate=pl.CostEstimate(
            flops=10 * work, bytes_accessed=8 * query.size, transcendentals=work // 64
        ),
    )(query, key, value, grad)


def pick(values, index):
    return lax.dynamic_index_in_dim(values, index, 0, keepdims=False)


def to_heads(chunks, own, size):
    slots = {0: pick(chunks, own)}
    for step in shift_order(size):
        chunk = pick(chunks, lax.rem(own + step, size))
        slots[step] = from_context(chunk, size - step, size)
    return jnp.stack([slots[step] for step in range(size)])


def to_frames(slots, own, size):
    arrived = {0: slots[0]}
    for step in shift_order(size):
        arrived[step] = from_context(slots[step], step, size)
    stacked = jnp.stack([arrived[step] for step in range(size)])
    return jnp.stack([pick(stacked, lax.rem(j - own + size, size)) for j in range(size)])


def relative_columns(own_fsdp, own_context, fsdp_size, context_size, width):
    block = width // (fsdp_size * context_size)
    there = lax.broadcasted_iota(jnp.int32, (width, width), 0)
    here = lax.broadcasted_iota(jnp.int32, (width, width), 1)
    far = lax.rem(here // (block * context_size) + own_fsdp, fsdp_size)
    step = lax.rem(lax.rem(here // block, context_size) + own_context, context_size)
    source = (far * context_size + step) * block + lax.rem(here, block)
    return (there == source).astype(low)


def on_device(sizes, frames, text_states, cotangent, *parameters):
    nf, nc, nt = sizes
    (
        self_query,
        self_key,
        self_value,
        self_out,
        cross_query,
        cross_key,
        cross_value,
        cross_out,
        feed_in,
        feed_out,
    ) = parameters[:10]
    own_fsdp = lax.axis_index("fsdp")
    own_context = lax.axis_index("context")
    own_tensor = lax.axis_index("tensor")
    frame_count, clips, features = frames.shape
    order = mask_order(nt)
    block = features // (nf * nc)
    columns = self_query.shape[1]
    halves = nc // clips
    width = columns // halves
    padded = -(-3 * width // 128) * 128
    gather = functools.partial(gather_group, fsdp_size=nf, context_size=nc)
    place = jnp.stack([own_context, own_tensor]).astype(jnp.int32)

    vectors = gather(jnp.stack(parameters[10:16] + parameters[10:12]), axis=1).astype(wide)
    pieces = []
    for part in range(halves):
        lanes = slice(part * width, (part + 1) * width)
        pieces += [self_query[:, lanes], self_key[:, lanes], self_value[:, lanes]]
        if padded > 3 * width:
            pieces.append(jnp.zeros((block, padded - 3 * width), low))
    qkv_all = gather(jnp.concatenate(pieces, axis=1))
    second_all = gather(jnp.concatenate([self_out, cross_query], axis=1))
    third_all = gather(jnp.concatenate([cross_key, cross_value, cross_out], axis=1))
    feed_in_all = gather(feed_in)
    feed_out_all = gather(feed_out)
    self_out_all, cross_query_all = second_all[:, :columns], second_all[:, columns:]
    cross_key_value = third_all[:, : 2 * columns]
    cross_out_all = third_all[:, 2 * columns :]

    relative = relative_columns(own_fsdp, own_context, nf, nc, features)
    residual = jnp.einsum("fcd,de->cfe", frames, relative, preferred_element_type=wide)
    incoming = jnp.einsum("fcd,de->cfe", cotangent, relative, preferred_element_type=wide)
    text = jnp.einsum("tcd,de->cte", text_states, relative, preferred_element_type=wide).astype(low)

    def by_row(values):
        return values.reshape(-1, values.shape[-1])

    def by_clip(values):
        return values.reshape(clips, -1, values.shape[-1])

    def to_chunks(values, lanes):
        parts = [values[..., j * lanes : (j + 1) * lanes] for j in range(halves)]
        return jnp.stack(parts, axis=1).reshape(clips * halves, values.shape[1], lanes)

    def from_chunks(chunks):
        chunks = chunks.reshape((clips, halves) + chunks.shape[1:])
        return jnp.concatenate([chunks[:, j] for j in range(halves)], axis=-1)

    normed_one = by_row(gather_rows(layer_norm(residual, vectors[0], vectors[1]), nt))
    projected = by_clip(dot(normed_one, qkv_all, 1, 0).astype(low))
    head_rows = to_heads(to_chunks(projected, padded), own_context, nc)
    head_out, head_top = self_forward(place, head_rows, width, frame_count, order)
    attended = by_row(from_chunks(to_frames(head_out, own_context, nc)))
    after_self = residual + scatter_rows(by_clip(dot(attended, self_out_all, 1, 1)), nt)

    normed_two = by_row(gather_rows(layer_norm(after_self, vectors[2], vectors[3]), nt))
    cross_queries = by_clip(dot(normed_two, cross_query_all, 1, 0).astype(low))
    text_projected = by_clip(dot(by_row(text), cross_key_value, 1, 0).astype(low))
    cross_keys, cross_values = text_projected[..., :columns], text_projected[..., columns:]
    crossed = cross_forward(cross_queries, cross_keys, cross_values)
    after_cross = after_self + scatter_rows(by_clip(dot(by_row(crossed), cross_out_all, 1, 1)), nt)

    normed_three = by_row(gather_rows(layer_norm(after_cross, vectors[4], vectors[5]), nt))
    hidden = dot(normed_three, feed_in_all, 1, 0)
    gate = 0.5 + 0.5 * lax.erf(hidden * (0.5**0.5))
    active = (hidden * gate).astype(low)
    layer_out = after_cross + scatter_rows(by_clip(dot(active, feed_out_all, 1, 1)), nt)
    layer_out = jnp.einsum("cfe,de->fcd", layer_out.astype(low), relative, preferred_element_type=wide).astype(low)

    grad_rows = by_row(gather_rows(incoming.astype(low), nt))
    grad_active = dot(grad_rows, feed_out_all, 1, 0)
    feed_out_grad = weight_grad(grad_rows, active, nf, nc)
    slope = gate + hidden * jnp.exp(-0.5 * hidden * hidden) * ((2.0 * jnp.pi) ** -0.5)
    grad_hidden = (grad_active * slope).astype(low)
    feed_in_grad = weight_grad(normed_three, grad_hidden, nf, nc)
    grad_normed = scatter_rows(by_clip(dot(grad_hidden, feed_in_all, 1, 1)), nt)
    piece, third_gain, third_shift = norm_back(after_cross, vectors[4], grad_normed)
    grad_after_cross = incoming + piece

    grad_rows = by_row(gather_rows(grad_after_cross.astype(low), nt))
    grad_crossed = by_clip(dot(grad_rows, cross_out_all, 1, 0).astype(low))
    cross_out_grad = weight_grad(grad_rows, by_row(crossed), nf, nc)
    grad_cross_queries, grad_cross_keys, grad_cross_values = cross_backward(
        cross_queries, cross_keys, cross_values, grad_crossed
    )
    grad_cross_queries = by_row(grad_cross_queries)
    cross_query_grad = weight_grad(normed_two, grad_cross_queries, nf, nc)
    grad_normed = scatter_rows(by_clip(dot(grad_cross_queries, cross_query_all, 1, 1)), nt)
    piece, second_gain, second_shift = norm_back(after_self, vectors[2], grad_normed)
    grad_after_self = grad_after_cross + piece

    text_grads = by_row(jnp.concatenate([grad_cross_keys, grad_cross_values], axis=-1))
    mask = 1
    while mask < nc:
        text_grads = text_grads + lax.ppermute(
            text_grads, "context", [(i, i ^ mask) for i in range(nc)]
        )
        mask *= 2
    text_low = text_grads.astype(low)
    near_columns = by_row(text[..., :block])
    far_blocks = [
        dot(by_row(text[..., far * nc * block : far * nc * block + block]), text_low, 0, 0).astype(low)
        for far in range(1, nf)
    ]
    key_value_grad = reduce_fsdp(dot(near_columns, text_low, 0, 0), far_blocks, nf)
    text_part = dot(text_low, cross_key_value, 1, 1)
    mask = 1
    while mask < nt:
        text_part = text_part + swap_tensor(text_part, mask, nt)
        mask *= 2
    text_grad = jnp.einsum(
        "cte,de->tcd", by_clip(text_part), relative.astype(wide), precision=lax.Precision.HIGHEST
    )

    grad_rows = by_row(gather_rows(grad_after_self.astype(low), nt))
    grad_attended = by_clip(dot(grad_rows, self_out_all, 1, 0).astype(low))
    self_out_grad = weight_grad(grad_rows, attended, nf, nc)
    head_grad = to_heads(to_chunks(grad_attended, width), own_context, nc)
    head_back = self_backward(place, head_rows, head_out, head_top, head_grad, frame_count, order)
    grad_projected = by_row(from_chunks(to_frames(head_back, own_context, nc)))
    qkv_grad = weight_grad(normed_one, grad_projected, nf, nc)
    grad_normed = scatter_rows(by_clip(dot(grad_projected, qkv_all, 1, 1)), nt)
    piece, first_gain, first_shift = norm_back(residual, vectors[0], grad_normed)
    frames_grad = jnp.einsum(
        "cfe,de->fcd",
        grad_after_self + piece,
        relative.astype(wide),
        precision=lax.Precision.HIGHEST,
    )

    norm_grads = jnp.stack(
        [first_gain, first_shift, second_gain, second_shift, third_gain, third_shift]
    )
    mask = 1
    while mask < nt:
        norm_grads = norm_grads + swap_tensor(norm_grads, mask, nt)
        mask *= 2
    half = nc * block
    total = norm_grads[:, :half]
    for step in range(1, nf):
        total = total + from_fsdp(norm_grads[:, step * half : (step + 1) * half], nf - step, nf)
    norm_result = total[:, :block]
    for step in shift_order(nc):
        norm_result = norm_result + from_context(
            total[:, step * block : (step + 1) * block], nc - step, nc
        )

    qkv_parts = []
    for kind in range(3):
        parts = [
            qkv_grad[:, part * padded + kind * width : part * padded + (kind + 1) * width]
            for part in range(halves)
        ]
        qkv_parts.append(jnp.concatenate(parts, axis=1))
    return (
        layer_out,
        frames_grad,
        text_grad,
        qkv_parts[0],
        qkv_parts[1],
        qkv_parts[2],
        self_out_grad,
        cross_query_grad,
        key_value_grad[:, :columns],
        key_value_grad[:, columns:],
        cross_out_grad,
        feed_in_grad,
        feed_out_grad,
        norm_result[0],
        norm_result[1],
        norm_result[2],
        norm_result[3],
        norm_result[4],
        norm_result[5],
    )


def solution(mesh):
    sizes = (mesh.shape["fsdp"], mesh.shape["context"], mesh.shape["tensor"])
    rows = P(("context", "tensor"), "fsdp", None)
    texts = P(None, "fsdp", None)
    matrix = P(("fsdp", "context"), "tensor")
    vector = P(("fsdp", "context"))
    return jax.shard_map(
        functools.partial(on_device, sizes),
        mesh=mesh,
        in_specs=(rows, texts, rows) + (matrix,) * 10 + (vector,) * 6,
        out_specs=(rows, rows, texts) + (matrix,) * 10 + (vector,) * 6,
        check_vma=False,
    )
```

```python
import functools

import jax
import jax.numpy as jnp
from jax import lax
from jax.experimental import pallas as pl
from jax.experimental.pallas import tpu as pltpu
from jax.sharding import PartitionSpec as P

HEAD = 64
low = jnp.bfloat16
wide = jnp.float32
masked_score = -1e30
scale = HEAD**-0.5


def dot(left, right, left_dim, right_dim):
    return lax.dot_general(
        left, right, (((left_dim,), (right_dim,)), ((), ())), preferred_element_type=wide
    )


def from_context(values, step, size):
    return lax.ppermute(values, "context", [((i + step) % size, i) for i in range(size)])


def from_fsdp(values, step, size):
    return lax.ppermute(values, "fsdp", [((i + step) % size, i) for i in range(size)])


def swap_tensor(values, mask, size):
    return lax.ppermute(values, "tensor", [(i, i ^ mask) for i in range(size)])


def shift_order(size):
    order = []
    for step in range(1, size // 2 + 1):
        order.append(step)
        if size - step != step:
            order.append(size - step)
    return order


def gather_group(shard, sizes, own):
    fsdp_size, context_size = sizes
    own_fsdp, own_context = own
    rows = shard.shape[0]
    pieces = [(0, 0, shard)]
    for far in range(1, fsdp_size):
        pieces.append((far, 0, from_fsdp(shard, far, fsdp_size)))
    for step in shift_order(context_size):
        arrived = from_context(shard, step, context_size)
        pieces.append((0, step, arrived))
        for far in range(1, fsdp_size):
            pieces.append((far, step, from_fsdp(arrived, far, fsdp_size)))
    result = jnp.zeros((fsdp_size * context_size,) + shard.shape, shard.dtype)
    for far, step, piece in pieces:
        index = lax.rem(own_fsdp + far, fsdp_size) * context_size + lax.rem(
            own_context + step, context_size
        )
        result = lax.dynamic_update_index_in_dim(result, piece, index, 0)
    return result.reshape((fsdp_size * context_size * rows,) + shard.shape[1:])


def reduce_group(parts, sizes, own):
    fsdp_size, context_size = sizes
    own_fsdp, own_context = own
    kind = low if parts.shape[1] * parts.shape[2] > 16384 else wide
    parts = parts.reshape((fsdp_size, context_size) + parts.shape[1:])
    total = pick(parts, own_fsdp)
    for step in range(1, fsdp_size):
        piece = pick(parts, lax.rem(own_fsdp + step, fsdp_size)).astype(kind)
        total = total + from_fsdp(piece, fsdp_size - step, fsdp_size).astype(wide)
    result = pick(total, own_context)
    for step in shift_order(context_size):
        piece = pick(total, lax.rem(own_context + step, context_size)).astype(kind)
        result = result + from_context(piece, context_size - step, context_size).astype(wide)
    return result


def pick(values, index):
    return lax.dynamic_index_in_dim(values, index, 0, keepdims=False)


def gather_rows(values, tensor_size):
    blocks = [values]
    mask = tensor_size // 2
    while mask:
        blocks = blocks + [swap_tensor(block, mask, tensor_size) for block in blocks]
        mask //= 2
    return jnp.concatenate(blocks, axis=1)


def mask_order(tensor_size):
    order = [0]
    mask = tensor_size // 2
    while mask:
        order = order + [item ^ mask for item in order]
        mask //= 2
    return order


def scatter_rows(parts, tensor_size):
    mask = 1
    while mask < tensor_size:
        half = parts.shape[1] // 2
        arrived = swap_tensor(parts[:, half:].astype(low), mask, tensor_size)
        parts = parts[:, :half] + arrived.astype(wide)
        mask *= 2
    return parts


def norm_stats(values):
    centre = jnp.mean(values, axis=-1, keepdims=True)
    centred = values - centre
    spread = jnp.mean(centred * centred, axis=-1, keepdims=True)
    root = lax.rsqrt(spread + 1e-05)
    return centred * root, root


def layer_norm(values, gain, shift):
    scaled, unused = norm_stats(values)
    return (scaled * gain + shift).astype(low)


def norm_back(values, gain, grad):
    scaled, root = norm_stats(values)
    weighted = grad * gain
    inner = jnp.mean(weighted * scaled, axis=-1, keepdims=True)
    outer = jnp.mean(weighted, axis=-1, keepdims=True)
    piece = root * (weighted - outer - scaled * inner)
    return piece, jnp.sum(grad * scaled, axis=(0, 1)), jnp.sum(grad, axis=(0, 1))


def frame_places(shape, axis, frames, order, own):
    row = lax.broadcasted_iota(jnp.int32, shape, axis)
    place = jnp.zeros(shape, jnp.int32)
    for slot, mask in enumerate(order):
        inside = (row >= slot * frames) & (row < (slot + 1) * frames)
        place = jnp.where(inside, (own ^ mask) * frames + row - slot * frames, place)
    return place


def fill_bias(bias_ref, frames, order, own):
    shape = bias_ref.shape
    keys = frame_places(shape, 0, frames, order, own)
    queries = frame_places(shape, 1, frames, order, own)
    bias_ref[...] = jnp.where(keys <= queries, 0.0, masked_score).astype(wide)


def self_forward_kernel(frames, order, place_ref, rows_ref, out_ref, top_ref, bias_ref):
    blocks, block_rows = rows_ref.shape[0], rows_ref.shape[1]
    width = out_ref.shape[2]
    heads = width // HEAD
    own_block = place_ref[0]
    fill_bias(bias_ref, frames, order, place_ref[1])

    def slot_of(block):
        return lax.rem(own_block - block + blocks, blocks)

    def query_block(block, unused):
        slot = slot_of(block)
        outs = []
        for head in range(heads):
            lanes = head * HEAD
            query = rows_ref[slot, :, lanes : lanes + HEAD] * scale

            def key_value(where, lanes=lanes):
                key = rows_ref[where, :, width + lanes : width + lanes + HEAD]
                value = rows_ref[where, :, 2 * width + lanes : 2 * width + lanes + HEAD]
                return key, value

            key, value = key_value(slot)
            scores = dot(key, query, 1, 1) + bias_ref[...]
            top = jnp.max(scores, axis=0, keepdims=True)
            weights = jnp.exp(scores - top)
            total = jnp.sum(weights, axis=0, keepdims=True)
            acc = dot(value, weights.astype(low), 0, 0)

            def step(past, carry, query=query, key_value=key_value):
                top, total, acc = carry
                key, value = key_value(slot_of(past))
                scores = dot(key, query, 1, 1)
                new_top = jnp.maximum(top, jnp.max(scores, axis=0, keepdims=True))
                weights = jnp.exp(scores - new_top)
                shrink = jnp.exp(top - new_top)
                total = total * shrink + jnp.sum(weights, axis=0, keepdims=True)
                acc = acc * shrink + dot(value, weights.astype(low), 0, 0)
                return new_top, total, acc

            top, total, acc = lax.fori_loop(0, block, step, (top, total, acc))
            outs.append((acc / total).T)
            top_ref[slot, head : head + 1, :] = top + jnp.log(total)
        out_ref[slot] = jnp.concatenate(outs, axis=1).astype(low)
        return unused

    lax.fori_loop(0, blocks, query_block, 0)


def self_backward_kernel(
    frames,
    order,
    place_ref,
    rows_ref,
    out_ref,
    top_ref,
    grad_ref,
    result_ref,
    bias_ref,
    delta_ref,
    query_acc,
    key_acc,
    value_acc,
):
    blocks, block_rows = rows_ref.shape[0], rows_ref.shape[1]
    width = out_ref.shape[2]
    heads = width // HEAD
    own_block = place_ref[0]
    fill_bias(bias_ref, frames, order, place_ref[1])
    query_acc[...] = jnp.zeros_like(query_acc)

    def slot_of(block):
        return lax.rem(own_block - block + blocks, blocks)

    def fill_delta(slot, unused):
        for head in range(heads):
            lanes = head * HEAD
            product = out_ref[slot, :, lanes : lanes + HEAD].astype(wide) * grad_ref[
                slot, :, lanes : lanes + HEAD
            ].astype(wide)
            delta_ref[slot, head : head + 1, :] = jnp.sum(product.T, axis=0, keepdims=True)
        return unused

    lax.fori_loop(0, blocks, fill_delta, 0)

    def key_block(block, unused):
        slot = slot_of(block)
        for head in range(heads):
            lanes = head * HEAD
            key = rows_ref[slot, :, width + lanes : width + lanes + HEAD]
            value = rows_ref[slot, :, 2 * width + lanes : 2 * width + lanes + HEAD]

            def terms(where, bias, lanes=lanes, head=head, key=key, value=value):
                query = rows_ref[where, :, lanes : lanes + HEAD] * scale
                grad = grad_ref[where, :, lanes : lanes + HEAD]
                scores = dot(key, query, 1, 1)
                if bias is not None:
                    scores = scores + bias
                weights = jnp.exp(scores - top_ref[where, head : head + 1, :])
                grad_weights = dot(value, grad, 1, 1)
                grad_scores = (weights * (grad_weights - delta_ref[where, head : head + 1, :])).astype(low)
                query_acc[head, where] += dot(key, grad_scores, 0, 0)
                return dot(grad_scores, query, 1, 0), dot(weights.astype(low), grad, 1, 0)

            start = terms(slot, bias_ref[...])

            def step(later, carry, terms=terms):
                key_part, value_part = terms(slot_of(later), None)
                return carry[0] + key_part, carry[1] + value_part

            key_grad, value_grad = lax.fori_loop(block + 1, blocks, step, start)
            key_acc[head, slot] = key_grad
            value_acc[head, slot] = value_grad
        return unused

    lax.fori_loop(0, blocks, key_block, 0)

    def write(slot, unused):
        parts = [(query_acc[head, slot] * scale).T for head in range(heads)]
        parts += [key_acc[head, slot] for head in range(heads)]
        parts += [value_acc[head, slot] for head in range(heads)]
        rest = result_ref.shape[2] - 3 * width
        if rest:
            parts.append(jnp.zeros((block_rows, rest), wide))
        result_ref[slot] = jnp.concatenate(parts, axis=1).astype(low)
        return unused

    lax.fori_loop(0, blocks, write, 0)


smem = pl.BlockSpec(memory_space=pltpu.SMEM)
vmem = pl.BlockSpec(memory_space=pltpu.VMEM)
kernel_params = pltpu.CompilerParams(vmem_limit_bytes=40 * 1024 * 1024)


def self_forward(place, rows, width, frames, order):
    blocks, block_rows, unused = rows.shape
    heads = width // HEAD
    work = blocks * block_rows * blocks * block_rows * heads * 5 // 8
    return pl.pallas_call(
        functools.partial(self_forward_kernel, frames, order),
        out_shape=(
            jax.ShapeDtypeStruct((blocks, block_rows, width), low),
            jax.ShapeDtypeStruct((blocks, heads, block_rows), wide),
        ),
        in_specs=[smem, vmem],
        out_specs=(vmem, vmem),
        scratch_shapes=[pltpu.VMEM((block_rows, block_rows), wide)],
        compiler_params=kernel_params,
        cost_estimate=pl.CostEstimate(
            flops=work * 64 * 4, bytes_accessed=rows.size * 4, transcendentals=work
        ),
    )(place, rows)


def self_backward(place, rows, out, top, grad, frames, order):
    blocks, block_rows, full = rows.shape
    width = out.shape[2]
    heads = width // HEAD
    work = blocks * block_rows * blocks * block_rows * heads * 5 // 8
    return pl.pallas_call(
        functools.partial(self_backward_kernel, frames, order),
        out_shape=jax.ShapeDtypeStruct((blocks, block_rows, full), low),
        in_specs=[smem, vmem, vmem, vmem, vmem],
        out_specs=vmem,
        scratch_shapes=[
            pltpu.VMEM((block_rows, block_rows), wide),
            pltpu.VMEM((blocks, heads, block_rows), wide),
            pltpu.VMEM((heads, blocks, HEAD, block_rows), wide),
            pltpu.VMEM((heads, blocks, block_rows, HEAD), wide),
            pltpu.VMEM((heads, blocks, block_rows, HEAD), wide),
        ],
        compiler_params=kernel_params,
        cost_estimate=pl.CostEstimate(
            flops=work * 64 * 10, bytes_accessed=rows.size * 8, transcendentals=work
        ),
    )(place, rows, out, top, grad)


def cross_weights(query, key):
    scores = dot(key, query * scale, 1, 1)
    top = jnp.max(scores, axis=0, keepdims=True)
    weights = jnp.exp(scores - top)
    return weights / jnp.sum(weights, axis=0, keepdims=True)


def cross_forward_kernel(query_ref, key_ref, value_ref, out_ref):
    outs = []
    for head in range(query_ref.shape[2] // HEAD):
        lanes = slice(head * HEAD, (head + 1) * HEAD)
        weights = cross_weights(query_ref[0, :, lanes], key_ref[0, :, lanes])
        outs.append(dot(value_ref[0, :, lanes], weights.astype(low), 0, 0).T)
    out_ref[0] = jnp.concatenate(outs, axis=1).astype(low)


def cross_backward_kernel(query_ref, key_ref, value_ref, grad_ref, query_out, key_out, value_out):
    queries, keys, values = [], [], []
    for head in range(query_ref.shape[2] // HEAD):
        lanes = slice(head * HEAD, (head + 1) * HEAD)
        query, key, value = query_ref[0, :, lanes], key_ref[0, :, lanes], value_ref[0, :, lanes]
        grad = grad_ref[0, :, lanes]
        weights = cross_weights(query, key)
        grad_weights = dot(value, grad, 1, 1)
        inner = jnp.sum(weights * grad_weights, axis=0, keepdims=True)
        grad_scores = (weights * (grad_weights - inner)).astype(low)
        queries.append((dot(key, grad_scores, 0, 0) * scale).T)
        keys.append(dot(grad_scores, query * scale, 1, 0))
        values.append(dot(weights.astype(low), grad, 1, 0))
    query_out[0] = jnp.concatenate(queries, axis=1).astype(low)
    key_out[0] = jnp.concatenate(keys, axis=1)
    value_out[0] = jnp.concatenate(values, axis=1)


def clip_spec(shape):
    return pl.BlockSpec((1,) + tuple(shape[1:]), lambda clip: (clip, 0, 0))


def cross_forward(query, key, value):
    work = query.shape[0] * query.shape[1] * query.shape[2] * key.shape[1]
    return pl.pallas_call(
        cross_forward_kernel,
        grid=(query.shape[0],),
        out_shape=jax.ShapeDtypeStruct(query.shape, low),
        in_specs=[clip_spec(query.shape), clip_spec(key.shape), clip_spec(value.shape)],
        out_specs=clip_spec(query.shape),
        compiler_params=kernel_params,
        cost_estimate=pl.CostEstimate(
            flops=4 * work, bytes_accessed=4 * query.size, transcendentals=work // 64
        ),
    )(query, key, value)


def cross_backward(query, key, value, grad):
    work = query.shape[0] * query.shape[1] * query.shape[2] * key.shape[1]
    return pl.pallas_call(
        cross_backward_kernel,
        grid=(query.shape[0],),
        out_shape=(
            jax.ShapeDtypeStruct(query.shape, low),
            jax.ShapeDtypeStruct(key.shape, wide),
            jax.ShapeDtypeStruct(value.shape, wide),
        ),
        in_specs=[
            clip_spec(query.shape),
            clip_spec(key.shape),
            clip_spec(value.shape),
            clip_spec(grad.shape),
        ],
        out_specs=(clip_spec(query.shape), clip_spec(key.shape), clip_spec(value.shape)),
        compiler_params=kernel_params,
        cost_estimate=pl.CostEstimate(
            flops=10 * work, bytes_accessed=8 * query.size, transcendentals=work // 64
        ),
    )(query, key, value, grad)


def to_heads(chunks, own, size):
    slots = {0: pick(chunks, own)}
    for step in shift_order(size):
        chunk = pick(chunks, lax.rem(own + step, size))
        slots[step] = from_context(chunk, size - step, size)
    return jnp.stack([slots[step] for step in range(size)])


def to_frames(slots, own, size):
    arrived = {0: slots[0]}
    for step in shift_order(size):
        arrived[step] = from_context(slots[step], step, size)
    stacked = jnp.stack([arrived[step] for step in range(size)])
    return jnp.stack([pick(stacked, lax.rem(j - own + size, size)) for j in range(size)])


def on_device(sizes, frames, text_states, cotangent, *parameters):
    nf, nc, nt = sizes
    (
        self_query,
        self_key,
        self_value,
        self_out,
        cross_query,
        cross_key,
        cross_value,
        cross_out,
        feed_in,
        feed_out,
    ) = parameters[:10]
    own_fsdp = lax.axis_index("fsdp")
    own_context = lax.axis_index("context")
    own_tensor = lax.axis_index("tensor")
    frame_count, clips, features = frames.shape
    order = mask_order(nt)
    block = features // (nf * nc)
    columns = self_query.shape[1]
    halves = nc // clips
    width = columns // halves
    padded = -(-3 * width // 128) * 128
    place = jnp.stack([own_context, own_tensor]).astype(jnp.int32)
    group = ((nf, nc), (own_fsdp, own_context))
    both = ("fsdp", "context")

    vectors = lax.all_gather(jnp.stack(parameters[10:16] + parameters[10:12]), both, axis=0)
    vectors = vectors.transpose(1, 0, 2).reshape(-1, features).astype(wide)
    pieces = []
    for part in range(halves):
        lanes = slice(part * width, (part + 1) * width)
        pieces += [self_query[:, lanes], self_key[:, lanes], self_value[:, lanes]]
        if padded > 3 * width:
            pieces.append(jnp.zeros((block, padded - 3 * width), low))
    qkv_all = gather_group(jnp.concatenate(pieces, axis=1), *group)
    second_all = gather_group(jnp.concatenate([self_out, cross_query], axis=1), *group)
    third_all = gather_group(jnp.concatenate([cross_key, cross_value, cross_out], axis=1), *group)
    feed_in_all = lax.all_gather(feed_in, both, axis=0, tiled=True)
    feed_out_all = lax.all_gather(feed_out, both, axis=0, tiled=True)
    self_out_all, cross_query_all = second_all[:, :columns], second_all[:, columns:]
    cross_key_value = third_all[:, : 2 * columns]
    cross_out_all = third_all[:, 2 * columns :]

    residual = frames.transpose(1, 0, 2).astype(wide)
    incoming = cotangent.transpose(1, 0, 2)
    text = text_states.transpose(1, 0, 2)

    def weight_grad(left_rows, right_rows):
        parts = dot(left_rows, right_rows, 0, 0).reshape(nf * nc, block, -1)
        return reduce_group(parts, *group)

    def feed_grad(left_rows, right_rows):
        parts = dot(left_rows, right_rows, 0, 0).astype(low)
        return lax.psum_scatter(parts, both, scatter_dimension=0, tiled=True).astype(wide)

    def by_row(values):
        return values.reshape(-1, values.shape[-1])

    def by_clip(values):
        return values.reshape(clips, -1, values.shape[-1])

    def to_chunks(values, lanes):
        parts = [values[..., j * lanes : (j + 1) * lanes] for j in range(halves)]
        return jnp.stack(parts, axis=1).reshape(clips * halves, values.shape[1], lanes)

    def from_chunks(chunks):
        chunks = chunks.reshape((clips, halves) + chunks.shape[1:])
        return jnp.concatenate([chunks[:, j] for j in range(halves)], axis=-1)

    normed_one = by_row(gather_rows(layer_norm(residual, vectors[0], vectors[1]), nt))
    projected = by_clip(dot(normed_one, qkv_all, 1, 0).astype(low))
    head_rows = to_heads(to_chunks(projected, padded), own_context, nc)
    head_out, head_top = self_forward(place, head_rows, width, frame_count, order)
    attended = by_row(from_chunks(to_frames(head_out, own_context, nc)))
    after_self = residual + scatter_rows(by_clip(dot(attended, self_out_all, 1, 1)), nt)

    normed_two = by_row(gather_rows(layer_norm(after_self, vectors[2], vectors[3]), nt))
    cross_queries = by_clip(dot(normed_two, cross_query_all, 1, 0).astype(low))
    text_projected = by_clip(dot(by_row(text), cross_key_value, 1, 0).astype(low))
    cross_keys, cross_values = text_projected[..., :columns], text_projected[..., columns:]
    crossed = cross_forward(cross_queries, cross_keys, cross_values)
    after_cross = after_self + scatter_rows(by_clip(dot(by_row(crossed), cross_out_all, 1, 1)), nt)

    normed_three = by_row(gather_rows(layer_norm(after_cross, vectors[4], vectors[5]), nt))
    hidden = dot(normed_three, feed_in_all, 1, 0)
    gate = 0.5 + 0.5 * lax.erf(hidden * (0.5**0.5))
    active = (hidden * gate).astype(low)
    layer_out = after_cross + scatter_rows(by_clip(dot(active, feed_out_all, 1, 1)), nt)
    layer_out = layer_out.astype(low).transpose(1, 0, 2)

    grad_rows = by_row(gather_rows(incoming, nt))
    grad_active = dot(grad_rows, feed_out_all, 1, 0)
    feed_out_grad = feed_grad(grad_rows, active)
    slope = gate + hidden * jnp.exp(-0.5 * hidden * hidden) * ((2.0 * jnp.pi) ** -0.5)
    grad_hidden = (grad_active * slope).astype(low)
    feed_in_grad = feed_grad(normed_three, grad_hidden)
    grad_normed = scatter_rows(by_clip(dot(grad_hidden, feed_in_all, 1, 1)), nt)
    piece, third_gain, third_shift = norm_back(after_cross, vectors[4], grad_normed)
    grad_after_cross = incoming.astype(wide) + piece

    grad_rows = by_row(gather_rows(grad_after_cross.astype(low), nt))
    grad_crossed = by_clip(dot(grad_rows, cross_out_all, 1, 0).astype(low))
    cross_out_grad = weight_grad(grad_rows, by_row(crossed))
    grad_cross_queries, grad_cross_keys, grad_cross_values = cross_backward(
        cross_queries, cross_keys, cross_values, grad_crossed
    )
    grad_cross_queries = by_row(grad_cross_queries)
    cross_query_grad = weight_grad(normed_two, grad_cross_queries)
    grad_normed = scatter_rows(by_clip(dot(grad_cross_queries, cross_query_all, 1, 1)), nt)
    piece, second_gain, second_shift = norm_back(after_self, vectors[2], grad_normed)
    grad_after_self = grad_after_cross + piece

    text_grads = by_row(jnp.concatenate([grad_cross_keys, grad_cross_values], axis=-1))
    mask = 1
    while mask < nc:
        text_grads = text_grads + lax.ppermute(
            text_grads, "context", [(i, i ^ mask) for i in range(nc)]
        )
        mask *= 2
    text_low = text_grads.astype(low)
    text_parts = dot(by_row(text), text_low, 0, 0).reshape(nf, nc, block, 2 * columns)
    key_value_grad = pick(pick(text_parts, own_fsdp), own_context)
    for step in range(1, nf):
        part = pick(pick(text_parts, lax.rem(own_fsdp + step, nf)), own_context).astype(low)
        key_value_grad = key_value_grad + from_fsdp(part, nf - step, nf).astype(wide)
    text_part = dot(text_low, cross_key_value, 1, 1)
    mask = 1
    while mask < nt:
        text_part = text_part + swap_tensor(text_part, mask, nt)
        mask *= 2
    text_grad = by_clip(text_part).transpose(1, 0, 2)

    grad_rows = by_row(gather_rows(grad_after_self.astype(low), nt))
    grad_attended = by_clip(dot(grad_rows, self_out_all, 1, 0).astype(low))
    self_out_grad = weight_grad(grad_rows, attended)
    head_grad = to_heads(to_chunks(grad_attended, width), own_context, nc)
    head_back = self_backward(place, head_rows, head_out, head_top, head_grad, frame_count, order)
    grad_projected = by_row(from_chunks(to_frames(head_back, own_context, nc)))
    qkv_grad = weight_grad(normed_one, grad_projected)
    grad_normed = scatter_rows(by_clip(dot(grad_projected, qkv_all, 1, 1)), nt)
    piece, first_gain, first_shift = norm_back(residual, vectors[0], grad_normed)
    frames_grad = (grad_after_self + piece).transpose(1, 0, 2)

    norm_grads = jnp.stack(
        [first_gain, first_shift, second_gain, second_shift, third_gain, third_shift]
    )
    mask = 1
    while mask < nt:
        norm_grads = norm_grads + swap_tensor(norm_grads, mask, nt)
        mask *= 2
    norm_parts = norm_grads.reshape(6, nf * nc, block).transpose(1, 0, 2)
    norm_result = reduce_group(norm_parts, *group)

    qkv_parts = []
    for kind in range(3):
        parts = [
            qkv_grad[:, part * padded + kind * width : part * padded + (kind + 1) * width]
            for part in range(halves)
        ]
        qkv_parts.append(jnp.concatenate(parts, axis=1))
    return (
        layer_out,
        frames_grad,
        text_grad,
        qkv_parts[0],
        qkv_parts[1],
        qkv_parts[2],
        self_out_grad,
        cross_query_grad,
        key_value_grad[:, :columns],
        key_value_grad[:, columns:],
        cross_out_grad,
        feed_in_grad,
        feed_out_grad,
        norm_result[0],
        norm_result[1],
        norm_result[2],
        norm_result[3],
        norm_result[4],
        norm_result[5],
    )


def solution(mesh):
    sizes = (mesh.shape["fsdp"], mesh.shape["context"], mesh.shape["tensor"])
    rows = P(("context", "tensor"), "fsdp", None)
    texts = P(None, "fsdp", None)
    matrix = P(("fsdp", "context"), "tensor")
    vector = P(("fsdp", "context"))
    return jax.shard_map(
        functools.partial(on_device, sizes),
        mesh=mesh,
        in_specs=(rows, texts, rows) + (matrix,) * 10 + (vector,) * 6,
        out_specs=(rows, rows, texts) + (matrix,) * 10 + (vector,) * 6,
        check_vma=False,
    )
```

```python
import functools

import jax
import jax.numpy as jnp
from jax import lax
from jax.experimental import pallas as pl
from jax.experimental.pallas import tpu as pltpu
from jax.experimental.layout import Layout, with_layout_constraint
from jax.sharding import PartitionSpec as P

HEAD = 64
low = jnp.bfloat16
wide = jnp.float32
masked_score = -1e30
scale = HEAD**-0.5


def dot(left, right, left_dim, right_dim):
    return lax.dot_general(
        left, right, (((left_dim,), (right_dim,)), ((), ())), preferred_element_type=wide
    )


def from_context(values, step, size):
    return lax.ppermute(values, "context", [((i + step) % size, i) for i in range(size)])


def from_fsdp(values, step, size):
    return lax.ppermute(values, "fsdp", [((i + step) % size, i) for i in range(size)])


def swap_tensor(values, mask, size):
    return lax.ppermute(values, "tensor", [(i, i ^ mask) for i in range(size)])


def shift_order(size):
    order = []
    for step in range(1, size // 2 + 1):
        order.append(step)
        if size - step != step:
            order.append(size - step)
    return order


def gather_group(shard, sizes, own):
    fsdp_size, context_size = sizes
    own_fsdp, own_context = own
    rows = shard.shape[0]
    pieces = [(0, 0, shard)]
    for far in range(1, fsdp_size):
        pieces.append((far, 0, from_fsdp(shard, far, fsdp_size)))
    for step in shift_order(context_size):
        arrived = from_context(shard, step, context_size)
        pieces.append((0, step, arrived))
        for far in range(1, fsdp_size):
            pieces.append((far, step, from_fsdp(arrived, far, fsdp_size)))
    result = jnp.zeros((fsdp_size * context_size,) + shard.shape, shard.dtype)
    for far, step, piece in pieces:
        index = lax.rem(own_fsdp + far, fsdp_size) * context_size + lax.rem(
            own_context + step, context_size
        )
        result = lax.dynamic_update_index_in_dim(result, piece, index, 0)
    return result.reshape((fsdp_size * context_size * rows,) + shard.shape[1:])


def reduce_group(parts, sizes, own):
    fsdp_size, context_size = sizes
    own_fsdp, own_context = own
    kind = low if parts.shape[1] * parts.shape[2] > 16384 else wide
    parts = parts.reshape((fsdp_size, context_size) + parts.shape[1:])
    total = pick(parts, own_fsdp)
    for step in range(1, fsdp_size):
        piece = pick(parts, lax.rem(own_fsdp + step, fsdp_size)).astype(kind)
        total = total + from_fsdp(piece, fsdp_size - step, fsdp_size).astype(wide)
    result = pick(total, own_context)
    for step in shift_order(context_size):
        piece = pick(total, lax.rem(own_context + step, context_size)).astype(kind)
        result = result + from_context(piece, context_size - step, context_size).astype(wide)
    return result


def pick_columns(values, index, count):
    span = values.shape[1] // count
    result = values[:, :span]
    for place in range(1, count):
        result = jnp.where(index == place, values[:, place * span : (place + 1) * span], result)
    return result


def pick(values, index):
    return lax.dynamic_index_in_dim(values, index, 0, keepdims=False)


def gather_rows(values, tensor_size):
    blocks = [values]
    mask = tensor_size // 2
    while mask:
        blocks = blocks + [swap_tensor(block, mask, tensor_size) for block in blocks]
        mask //= 2
    return jnp.concatenate(blocks, axis=1)


def mask_order(tensor_size):
    order = [0]
    mask = tensor_size // 2
    while mask:
        order = order + [item ^ mask for item in order]
        mask //= 2
    return order


def scatter_rows(parts, tensor_size, first=1):
    mask = first
    while mask < tensor_size:
        parts = scatter_step(parts, mask, tensor_size)
        mask *= 2
    return parts


def scatter_step(parts, mask, tensor_size):
    half = parts.shape[1] // 2
    arrived = swap_tensor(parts[:, half:].astype(low), mask, tensor_size)
    return parts[:, :half] + arrived.astype(wide)


def norm_stats(values):
    centre = jnp.mean(values, axis=-1, keepdims=True)
    centred = values - centre
    spread = jnp.mean(centred * centred, axis=-1, keepdims=True)
    root = lax.rsqrt(spread + 1e-05)
    return centred * root, root


def layer_norm(values, gain, shift):
    scaled, unused = norm_stats(values)
    return (scaled * gain + shift).astype(low)


def norm_back(values, gain, grad):
    scaled, root = norm_stats(values)
    weighted = grad * gain
    inner = jnp.mean(weighted * scaled, axis=-1, keepdims=True)
    outer = jnp.mean(weighted, axis=-1, keepdims=True)
    piece = root * (weighted - outer - scaled * inner)
    return piece, jnp.sum(grad * scaled, axis=(0, 1)), jnp.sum(grad, axis=(0, 1))


def frame_places(shape, axis, frames, order, own):
    row = lax.broadcasted_iota(jnp.int32, shape, axis)
    place = jnp.zeros(shape, jnp.int32)
    for slot, mask in enumerate(order):
        inside = (row >= slot * frames) & (row < (slot + 1) * frames)
        place = jnp.where(inside, (own ^ mask) * frames + row - slot * frames, place)
    return place


def fill_bias(bias_ref, frames, order, own):
    shape = bias_ref.shape
    keys = frame_places(shape, 0, frames, order, own)
    queries = frame_places(shape, 1, frames, order, own)
    bias_ref[...] = jnp.where(keys <= queries, 0.0, masked_score).astype(wide)


def self_forward_kernel(frames, order, place_ref, rows_ref, out_ref, top_ref, bias_ref):
    blocks, block_rows = rows_ref.shape[0], rows_ref.shape[1]
    width = out_ref.shape[2]
    heads = width // HEAD
    own_block = place_ref[0]
    fill_bias(bias_ref, frames, order, place_ref[1])

    def slot_of(block):
        return lax.rem(own_block - block + blocks, blocks)

    def query_block(block, unused):
        slot = slot_of(block)
        outs = []
        for head in range(heads):
            lanes = head * HEAD
            query = rows_ref[slot, :, lanes : lanes + HEAD] * scale

            def key_value(where, lanes=lanes):
                key = rows_ref[where, :, width + lanes : width + lanes + HEAD]
                value = rows_ref[where, :, 2 * width + lanes : 2 * width + lanes + HEAD]
                return key, value

            key, value = key_value(slot)
            scores = dot(key, query, 1, 1) + bias_ref[...]
            top = jnp.max(scores, axis=0, keepdims=True)
            weights = jnp.exp(scores - top)
            total = jnp.sum(weights, axis=0, keepdims=True)
            acc = dot(value, weights.astype(low), 0, 0)

            def step(past, carry, query=query, key_value=key_value):
                top, total, acc = carry
                key, value = key_value(slot_of(past))
                scores = dot(key, query, 1, 1)
                new_top = jnp.maximum(top, jnp.max(scores, axis=0, keepdims=True))
                weights = jnp.exp(scores - new_top)
                shrink = jnp.exp(top - new_top)
                total = total * shrink + jnp.sum(weights, axis=0, keepdims=True)
                acc = acc * shrink + dot(value, weights.astype(low), 0, 0)
                return new_top, total, acc

            top, total, acc = lax.fori_loop(0, block, step, (top, total, acc))
            outs.append((acc / total).T)
            top_ref[slot, head : head + 1, :] = top + jnp.log(total)
        out_ref[slot] = jnp.concatenate(outs, axis=1).astype(low)
        return unused

    lax.fori_loop(0, blocks, query_block, 0)


def self_backward_kernel(
    frames,
    order,
    place_ref,
    rows_ref,
    out_ref,
    top_ref,
    grad_ref,
    result_ref,
    bias_ref,
    delta_ref,
    query_acc,
    key_acc,
    value_acc,
):
    blocks, block_rows = rows_ref.shape[0], rows_ref.shape[1]
    width = out_ref.shape[2]
    heads = width // HEAD
    own_block = place_ref[0]
    fill_bias(bias_ref, frames, order, place_ref[1])
    query_acc[...] = jnp.zeros_like(query_acc)

    def slot_of(block):
        return lax.rem(own_block - block + blocks, blocks)

    def fill_delta(slot, unused):
        for head in range(heads):
            lanes = head * HEAD
            product = out_ref[slot, :, lanes : lanes + HEAD].astype(wide) * grad_ref[
                slot, :, lanes : lanes + HEAD
            ].astype(wide)
            delta_ref[slot, head : head + 1, :] = jnp.sum(product.T, axis=0, keepdims=True)
        return unused

    lax.fori_loop(0, blocks, fill_delta, 0)

    def key_block(block, unused):
        slot = slot_of(block)
        for head in range(heads):
            lanes = head * HEAD
            key = rows_ref[slot, :, width + lanes : width + lanes + HEAD]
            value = rows_ref[slot, :, 2 * width + lanes : 2 * width + lanes + HEAD]

            def terms(where, bias, lanes=lanes, head=head, key=key, value=value):
                query = rows_ref[where, :, lanes : lanes + HEAD] * scale
                grad = grad_ref[where, :, lanes : lanes + HEAD]
                scores = dot(key, query, 1, 1)
                if bias is not None:
                    scores = scores + bias
                weights = jnp.exp(scores - top_ref[where, head : head + 1, :])
                grad_weights = dot(value, grad, 1, 1)
                grad_scores = (weights * (grad_weights - delta_ref[where, head : head + 1, :])).astype(low)
                query_acc[head, where] += dot(key, grad_scores, 0, 0)
                return dot(grad_scores, query, 1, 0), dot(weights.astype(low), grad, 1, 0)

            start = terms(slot, bias_ref[...])

            def step(later, carry, terms=terms):
                key_part, value_part = terms(slot_of(later), None)
                return carry[0] + key_part, carry[1] + value_part

            key_grad, value_grad = lax.fori_loop(block + 1, blocks, step, start)
            key_acc[head, slot] = key_grad
            value_acc[head, slot] = value_grad
        return unused

    lax.fori_loop(0, blocks, key_block, 0)

    def write(slot, unused):
        parts = [(query_acc[head, slot] * scale).T for head in range(heads)]
        parts += [key_acc[head, slot] for head in range(heads)]
        parts += [value_acc[head, slot] for head in range(heads)]
        rest = result_ref.shape[2] - 3 * width
        if rest:
            parts.append(jnp.zeros((block_rows, rest), wide))
        result_ref[slot] = jnp.concatenate(parts, axis=1).astype(low)
        return unused

    lax.fori_loop(0, blocks, write, 0)


smem = pl.BlockSpec(memory_space=pltpu.SMEM)
vmem = pl.BlockSpec(memory_space=pltpu.VMEM)
kernel_params = pltpu.CompilerParams(vmem_limit_bytes=40 * 1024 * 1024)


def self_forward(place, rows, width, frames, order):
    blocks, block_rows, unused = rows.shape
    heads = width // HEAD
    work = blocks * block_rows * blocks * block_rows * heads * 5 // 8
    return pl.pallas_call(
        functools.partial(self_forward_kernel, frames, order),
        out_shape=(
            jax.ShapeDtypeStruct((blocks, block_rows, width), low),
            jax.ShapeDtypeStruct((blocks, heads, block_rows), wide),
        ),
        in_specs=[smem, vmem],
        out_specs=(vmem, vmem),
        scratch_shapes=[pltpu.VMEM((block_rows, block_rows), wide)],
        compiler_params=kernel_params,
        cost_estimate=pl.CostEstimate(
            flops=work * 64 * 4, bytes_accessed=rows.size * 4, transcendentals=work
        ),
    )(place, rows)


def self_backward(place, rows, out, top, grad, frames, order):
    blocks, block_rows, full = rows.shape
    width = out.shape[2]
    heads = width // HEAD
    work = blocks * block_rows * blocks * block_rows * heads * 5 // 8
    return pl.pallas_call(
        functools.partial(self_backward_kernel, frames, order),
        out_shape=jax.ShapeDtypeStruct((blocks, block_rows, full), low),
        in_specs=[smem, vmem, vmem, vmem, vmem],
        out_specs=vmem,
        scratch_shapes=[
            pltpu.VMEM((block_rows, block_rows), wide),
            pltpu.VMEM((blocks, heads, block_rows), wide),
            pltpu.VMEM((heads, blocks, HEAD, block_rows), wide),
            pltpu.VMEM((heads, blocks, block_rows, HEAD), wide),
            pltpu.VMEM((heads, blocks, block_rows, HEAD), wide),
        ],
        compiler_params=kernel_params,
        cost_estimate=pl.CostEstimate(
            flops=work * 64 * 10, bytes_accessed=rows.size * 8, transcendentals=work
        ),
    )(place, rows, out, top, grad)


def cross_weights(query, key):
    scores = dot(key, query * scale, 1, 1)
    top = jnp.max(scores, axis=0, keepdims=True)
    weights = jnp.exp(scores - top)
    return weights / jnp.sum(weights, axis=0, keepdims=True)


def cross_forward_kernel(query_ref, key_ref, value_ref, out_ref):
    outs = []
    for head in range(query_ref.shape[2] // HEAD):
        lanes = slice(head * HEAD, (head + 1) * HEAD)
        weights = cross_weights(query_ref[0, :, lanes], key_ref[0, :, lanes])
        outs.append(dot(value_ref[0, :, lanes], weights.astype(low), 0, 0).T)
    out_ref[0] = jnp.concatenate(outs, axis=1).astype(low)


def cross_backward_kernel(query_ref, key_ref, value_ref, grad_ref, query_out, key_out, value_out):
    queries, keys, values = [], [], []
    for head in range(query_ref.shape[2] // HEAD):
        lanes = slice(head * HEAD, (head + 1) * HEAD)
        query, key, value = query_ref[0, :, lanes], key_ref[0, :, lanes], value_ref[0, :, lanes]
        grad = grad_ref[0, :, lanes]
        weights = cross_weights(query, key)
        grad_weights = dot(value, grad, 1, 1)
        inner = jnp.sum(weights * grad_weights, axis=0, keepdims=True)
        grad_scores = (weights * (grad_weights - inner)).astype(low)
        queries.append((dot(key, grad_scores, 0, 0) * scale).T)
        keys.append(dot(grad_scores, query * scale, 1, 0))
        values.append(dot(weights.astype(low), grad, 1, 0))
    query_out[0] = jnp.concatenate(queries, axis=1).astype(low)
    key_out[0] = jnp.concatenate(keys, axis=1)
    value_out[0] = jnp.concatenate(values, axis=1)


def clip_spec(shape):
    return pl.BlockSpec((1,) + tuple(shape[1:]), lambda clip: (clip, 0, 0))


def cross_forward(query, key, value):
    work = query.shape[0] * query.shape[1] * query.shape[2] * key.shape[1]
    return pl.pallas_call(
        cross_forward_kernel,
        grid=(query.shape[0],),
        out_shape=jax.ShapeDtypeStruct(query.shape, low),
        in_specs=[clip_spec(query.shape), clip_spec(key.shape), clip_spec(value.shape)],
        out_specs=clip_spec(query.shape),
        compiler_params=kernel_params,
        cost_estimate=pl.CostEstimate(
            flops=4 * work, bytes_accessed=4 * query.size, transcendentals=work // 64
        ),
    )(query, key, value)


def cross_backward(query, key, value, grad):
    work = query.shape[0] * query.shape[1] * query.shape[2] * key.shape[1]
    return pl.pallas_call(
        cross_backward_kernel,
        grid=(query.shape[0],),
        out_shape=(
            jax.ShapeDtypeStruct(query.shape, low),
            jax.ShapeDtypeStruct(key.shape, wide),
            jax.ShapeDtypeStruct(value.shape, wide),
        ),
        in_specs=[
            clip_spec(query.shape),
            clip_spec(key.shape),
            clip_spec(value.shape),
            clip_spec(grad.shape),
        ],
        out_specs=(clip_spec(query.shape), clip_spec(key.shape), clip_spec(value.shape)),
        compiler_params=kernel_params,
        cost_estimate=pl.CostEstimate(
            flops=10 * work, bytes_accessed=8 * query.size, transcendentals=work // 64
        ),
    )(query, key, value, grad)


def to_heads(chunks, own, size):
    slots = {0: pick(chunks, own)}
    for step in shift_order(size):
        chunk = pick(chunks, lax.rem(own + step, size))
        slots[step] = from_context(chunk, size - step, size)
    return jnp.stack([slots[step] for step in range(size)])


def to_frames(slots, own, size):
    arrived = {0: slots[0]}
    for step in shift_order(size):
        arrived[step] = from_context(slots[step], step, size)
    stacked = jnp.stack([arrived[step] for step in range(size)])
    return jnp.stack([pick(stacked, lax.rem(j - own + size, size)) for j in range(size)])


def on_device(sizes, frames, text_states, cotangent, *parameters):
    nf, nc, nt = sizes
    (
        self_query,
        self_key,
        self_value,
        self_out,
        cross_query,
        cross_key,
        cross_value,
        cross_out,
        feed_in,
        feed_out,
    ) = parameters[:10]
    own_fsdp = lax.axis_index("fsdp")
    own_context = lax.axis_index("context")
    own_tensor = lax.axis_index("tensor")
    frame_count, clips, features = frames.shape
    order = mask_order(nt)
    block = features // (nf * nc)
    columns = self_query.shape[1]
    halves = nc // clips
    width = columns // halves
    padded = 3 * width
    place = jnp.stack([own_context, own_tensor]).astype(jnp.int32)
    group = ((nf, nc), (own_fsdp, own_context))
    both = ("fsdp", "context")

    def gather_calls(shard):
        return lax.all_gather(shard, both, axis=0, tiled=True)

    vectors = gather_group(jnp.stack(parameters[10:16] + parameters[10:12]), *group)
    vectors = vectors.reshape(nf * nc, -1, block).transpose(1, 0, 2).reshape(-1, features)
    vectors = vectors.astype(wide)
    pieces = []
    for part in range(halves):
        lanes = slice(part * width, (part + 1) * width)
        pieces += [self_query[:, lanes], self_key[:, lanes], self_value[:, lanes]]
    qkv_all = gather_group(jnp.concatenate(pieces, axis=1), *group)
    second_all = gather_calls(jnp.concatenate([cross_query, cross_out], axis=1))
    third_all = gather_calls(jnp.concatenate([self_out, cross_key, cross_value], axis=1))
    feed_in_near = lax.all_gather(feed_in, "context", axis=0, tiled=True)
    feed_out_all = gather_calls(feed_out)
    self_out_all = third_all[:, :columns]
    cross_key_value = third_all[:, columns:]

    def gather_columns(blocks, first, last):
        mask = first
        while mask >= last:
            blocks = blocks + [swap_tensor(part, mask, nt) for part in blocks]
            mask //= 2
        return blocks

    def side_by_side(blocks):
        return [
            jnp.concatenate([part[:, side * columns : (side + 1) * columns] for part in blocks], axis=1)
            for side in range(2)
        ]

    def scatter_columns(parts, mask=1):
        while mask < nt:
            half = parts.shape[-1] // 2
            arrived = swap_tensor(parts[..., half:].astype(low), mask, nt)
            parts = parts[..., :half] + arrived.astype(wide)
            mask *= 2
        return parts

    def row_major(values):
        return with_layout_constraint(values, Layout(major_to_minor=(0, 1)))

    def outer_start(*products):
        half = products[0][1].shape[1] // 2
        far = [row_major(dot(left, right[:, half:], 0, 0)).astype(low) for left, right in products]
        near = [row_major(dot(left, right[:, :half], 0, 0)) for left, right in products]
        return near + [swap_tensor(jnp.concatenate(far, axis=1), 1, nt)]

    def outer_step(near, arrived):
        span = near[0].shape[1]
        return [
            part + arrived[:, k * span : (k + 1) * span].astype(wide) for k, part in enumerate(near)
        ]

    def outer_rest(near, arrived):
        near = outer_step(near, arrived)
        mask = 2
        while mask < nt:
            half = near[0].shape[1] // 2
            far = jnp.concatenate([part[:, half:].astype(low) for part in near], axis=1)
            far = swap_tensor(far, mask, nt)
            near = [part[:, :half] for part in near]
            mask *= 2
            if mask < nt:
                near = outer_step(near, far)
        return near + [far]


    residual = frames.transpose(1, 0, 2).astype(wide)
    incoming = cotangent.transpose(1, 0, 2)
    text = text_states.transpose(1, 0, 2)

    def after(*values):
        return lax.optimization_barrier(values)

    def grad_start(*products):
        def block_of(index):
            parts = [
                with_layout_constraint(
                    dot(pick_columns(left, index, nf), right, 0, 0), Layout(major_to_minor=(0, 1))
                )
                for left, right in products
            ]
            return parts[0] if len(parts) == 1 else jnp.concatenate(parts, axis=1)

        far = [
            from_fsdp(block_of(lax.rem(own_fsdp + step, nf)).astype(low), nf - step, nf)
            for step in range(1, nf)
        ]
        return [block_of(own_fsdp)] + far

    def block_sum(blocks):
        total = blocks[0]
        for piece in blocks[1:]:
            total = total + piece.astype(wide)
        return total

    def grad_scatter(total):
        return lax.psum_scatter(total, "context", scatter_dimension=0, tiled=True)

    def grad_finish(blocks):
        return grad_scatter(block_sum(blocks).astype(low))

    def by_row(values):
        return values.reshape(-1, values.shape[-1])

    def by_clip(values):
        return values.reshape(clips, -1, values.shape[-1])

    def to_chunks(values, lanes):
        parts = [values[..., j * lanes : (j + 1) * lanes] for j in range(halves)]
        return jnp.stack(parts, axis=1).reshape(clips * halves, values.shape[1], lanes)

    def from_chunks(chunks):
        chunks = chunks.reshape((clips, halves) + chunks.shape[1:])
        return jnp.concatenate([chunks[:, j] for j in range(halves)], axis=-1)

    normed_one = by_row(gather_rows(layer_norm(residual, vectors[0], vectors[1]), nt))
    normed_one, second_all = after(normed_one, second_all)
    second_blocks = gather_columns([second_all], nt // 2, 2)
    projected = by_clip(dot(normed_one, qkv_all, 1, 0).astype(low))
    head_rows = to_heads(to_chunks(projected, padded), own_context, nc)
    head_rows, *second_blocks = after(head_rows, *second_blocks)
    head_out, head_top = self_forward(place, head_rows, width, frame_count, order)
    head_out, cross_key_value, *second_blocks = after(head_out, cross_key_value, *second_blocks)
    cross_query_all, cross_out_all = side_by_side(gather_columns(second_blocks, 1, 1))
    attended = by_row(from_chunks(to_frames(head_out, own_context, nc)))
    text_projected = dot(by_row(text), cross_key_value, 1, 0).astype(low)
    cross_keys, cross_values = [
        by_clip(part) for part in side_by_side(gather_columns([text_projected], nt // 2, 1))
    ]
    attended, cross_keys, cross_values, feed_in_near = after(
        attended, cross_keys, cross_values, feed_in_near
    )
    feed_in_pieces = [feed_in_near] + [from_fsdp(feed_in_near, far, nf) for far in range(1, nf)]
    after_self = residual + scatter_rows(by_clip(dot(attended, self_out_all, 1, 1)), nt)

    normed_two = by_row(layer_norm(after_self, vectors[2], vectors[3]))
    cross_queries = by_clip(dot(normed_two, cross_query_all, 1, 0).astype(low))
    crossed = cross_forward(cross_queries, cross_keys, cross_values)
    after_cross = after_self + by_clip(dot(by_row(crossed), cross_out_all, 1, 1))

    normed_three = by_row(gather_rows(layer_norm(after_cross, vectors[4], vectors[5]), nt))
    normed_three, *feed_in_pieces = after(normed_three, *feed_in_pieces)
    feed_in_all = jnp.zeros((nf,) + feed_in_near.shape, low)
    for far, piece in enumerate(feed_in_pieces):
        feed_in_all = lax.dynamic_update_index_in_dim(
            feed_in_all, piece, lax.rem(own_fsdp + far, nf), 0
        )
    feed_in_all = feed_in_all.reshape(features, -1)
    hidden = dot(normed_three, feed_in_all, 1, 0)
    gate = 0.5 + 0.5 * lax.erf(hidden * (0.5**0.5))
    active = (hidden * gate).astype(low)
    layer_out = after_cross + scatter_rows(by_clip(dot(active, feed_out_all, 1, 1)), nt)
    layer_out = layer_out.astype(low).transpose(1, 0, 2)

    grad_rows = by_row(gather_rows(incoming, nt))
    grad_active = dot(grad_rows, feed_out_all, 1, 0)
    feed_out_blocks = grad_start((grad_rows, active))
    slope = gate + hidden * jnp.exp(-0.5 * hidden * hidden) * ((2.0 * jnp.pi) ** -0.5)
    grad_hidden = (grad_active * slope).astype(low)
    grad_normed = scatter_rows(by_clip(dot(grad_hidden, feed_in_all, 1, 1)), nt)
    piece, third_gain, third_shift = norm_back(after_cross, vectors[4], grad_normed)
    grad_after_cross = incoming.astype(wide) + piece

    cross_rows = by_row(grad_after_cross.astype(low))
    grad_crossed = by_clip(dot(cross_rows, cross_out_all, 1, 0).astype(low))
    grad_cross_queries, grad_cross_keys, grad_cross_values = cross_backward(
        cross_queries, cross_keys, cross_values, grad_crossed
    )
    grad_cross_queries = by_row(grad_cross_queries)
    grad_normed = by_clip(dot(grad_cross_queries, cross_query_all, 1, 1))
    piece, second_gain, second_shift = norm_back(after_self, vectors[2], grad_normed)
    grad_after_self = grad_after_cross + piece
    grad_after_self, normed_three, grad_hidden = after(grad_after_self, normed_three, grad_hidden)
    feed_in_blocks = grad_start((normed_three, grad_hidden))
    cross_parts = outer_start((cross_rows, by_row(crossed)), (normed_two, grad_cross_queries))

    def text_sum(values, mask):
        arrived = lax.ppermute(values.astype(low), "context", [(i, i ^ mask) for i in range(nc)])
        return values + arrived.astype(wide)

    text_grads = scatter_columns(jnp.stack([by_row(grad_cross_keys), by_row(grad_cross_values)]))
    text_grads = jnp.concatenate([text_grads[0], text_grads[1]], axis=1)
    mask = 1
    while 2 * mask < nc:
        text_grads = text_sum(text_grads, mask)
        mask *= 2
    grad_rows = by_row(gather_rows(grad_after_self.astype(low), nt))
    grad_rows, text_grads, *feed_out_blocks = after(grad_rows, text_grads, *feed_out_blocks)
    feed_out_grad = grad_finish(feed_out_blocks)
    text_grads = text_sum(text_grads, mask)

    grad_attended = by_clip(dot(grad_rows, self_out_all, 1, 0).astype(low))
    grad_attended, *cross_parts = after(grad_attended, *cross_parts)
    cross_parts = outer_rest(cross_parts[:2], cross_parts[2])
    self_out_blocks = grad_start((grad_rows, attended))
    head_grad = to_heads(to_chunks(grad_attended, width), own_context, nc)
    head_grad, text_grads, feed_out_grad, *feed_in_blocks = after(
        head_grad, text_grads, feed_out_grad, *feed_in_blocks
    )
    feed_in_grad = grad_finish(feed_in_blocks)
    feed_out_grad = feed_out_grad.astype(wide)
    head_back = self_backward(place, head_rows, head_out, head_top, head_grad, frame_count, order)
    head_back, *cross_parts = after(head_back, *cross_parts)
    cross_parts = outer_step(cross_parts[:2], cross_parts[2])

    def cross_block(index):
        span = nc * block
        picked = []
        for part in cross_parts:
            chosen = part[:span]
            for where in range(1, nf):
                chosen = jnp.where(index == where, part[where * span : (where + 1) * span], chosen)
            picked.append(chosen)
        return jnp.concatenate(picked, axis=1)

    cross_blocks = [cross_block(own_fsdp)] + [
        from_fsdp(cross_block(lax.rem(own_fsdp + step, nf)).astype(low), nf - step, nf)
        for step in range(1, nf)
    ]
    text_low = text_grads.astype(low)
    def text_block(step):
        place = lax.rem(own_fsdp + step, nf) * nc + own_context
        return dot(pick_columns(by_row(text), place, nf * nc), text_low, 0, 0)

    text_blocks = [text_block(0)] + [
        from_fsdp(text_block(step).astype(low), nf - step, nf) for step in range(1, nf)
    ]
    text_part = dot(text_low, cross_key_value, 1, 1)
    mask = 1
    while mask < nt:
        text_part = text_part + swap_tensor(text_part.astype(low), mask, nt).astype(wide)
        mask *= 2

    grad_projected = by_row(from_chunks(to_frames(head_back, own_context, nc)))
    count = len(cross_blocks)
    grad_projected, feed_in_grad, text_part, *moved = after(
        grad_projected, feed_in_grad, text_part, *cross_blocks, *self_out_blocks, *text_blocks
    )
    middle_total = [block_sum(moved[:count]).astype(low), block_sum(moved[count : 2 * count]).astype(low)]
    middle_grad = grad_scatter(jnp.concatenate(middle_total, axis=1))
    text_blocks = moved[2 * count :]
    key_value_grad = block_sum(text_blocks)
    text_grad = by_clip(text_part).transpose(1, 0, 2)
    feed_in_grad = feed_in_grad.astype(wide)
    cut = grad_projected.shape[1] // 256 * 128 + 128
    early = grad_start((normed_one, grad_projected[:, :cut]))
    late = grad_start((normed_one, grad_projected[:, cut:]))
    grad_normed = scatter_step(by_clip(dot(grad_projected, qkv_all, 1, 1)), 1, nt)
    grad_normed, middle_grad, *early = after(grad_normed, middle_grad, *early)
    early = grad_finish(early)
    grad_normed = scatter_rows(grad_normed, nt, 2)
    grad_normed, *late = after(grad_normed, *late)
    qkv_grad = jnp.concatenate([early.astype(wide), grad_finish(late).astype(wide)], axis=1)
    middle_grad = middle_grad.astype(wide)
    cross_out_grad = middle_grad[:, :columns]
    cross_query_grad = middle_grad[:, columns : 2 * columns]
    self_out_grad = middle_grad[:, 2 * columns :]
    piece, first_gain, first_shift = norm_back(residual, vectors[0], grad_normed)
    frames_grad = (grad_after_self + piece).transpose(1, 0, 2)

    norm_grads = jnp.stack(
        [first_gain, first_shift, second_gain, second_shift, third_gain, third_shift]
    )
    mask = 1
    while mask < nt:
        norm_grads = norm_grads + swap_tensor(norm_grads, mask, nt)
        mask *= 2
    norm_parts = norm_grads.reshape(6, nf * nc, block).transpose(1, 0, 2)
    norm_result = reduce_group(norm_parts, *group)

    qkv_parts = []
    for kind in range(3):
        parts = [
            qkv_grad[:, part * padded + kind * width : part * padded + (kind + 1) * width]
            for part in range(halves)
        ]
        qkv_parts.append(jnp.concatenate(parts, axis=1))
    return (
        layer_out,
        frames_grad,
        text_grad,
        qkv_parts[0],
        qkv_parts[1],
        qkv_parts[2],
        self_out_grad,
        cross_query_grad,
        key_value_grad[:, :columns],
        key_value_grad[:, columns:],
        cross_out_grad,
        feed_in_grad,
        feed_out_grad,
        norm_result[0],
        norm_result[1],
        norm_result[2],
        norm_result[3],
        norm_result[4],
        norm_result[5],
    )


def solution(mesh):
    sizes = (mesh.shape["fsdp"], mesh.shape["context"], mesh.shape["tensor"])
    rows = P(("context", "tensor"), "fsdp", None)
    texts = P(None, "fsdp", None)
    matrix = P(("fsdp", "context"), "tensor")
    vector = P(("fsdp", "context"))
    return jax.shard_map(
        functools.partial(on_device, sizes),
        mesh=mesh,
        in_specs=(rows, texts, rows) + (matrix,) * 10 + (vector,) * 6,
        out_specs=(rows, rows, texts) + (matrix,) * 10 + (vector,) * 6,
        check_vma=False,
    )
```

```python
import functools

import jax
import jax.numpy as jnp
from jax import lax
from jax.experimental import pallas as pl
from jax.experimental.pallas import tpu as pltpu
from jax.experimental.layout import Layout, with_layout_constraint
from jax.sharding import PartitionSpec as P

HEAD = 64
low = jnp.bfloat16
wide = jnp.float32
masked_score = -1e30
scale = HEAD**-0.5


def dot(left, right, left_dim, right_dim):
    return lax.dot_general(
        left, right, (((left_dim,), (right_dim,)), ((), ())), preferred_element_type=wide
    )


def from_context(values, step, size):
    return lax.ppermute(values, "context", [((i + step) % size, i) for i in range(size)])


def from_fsdp(values, step, size):
    return lax.ppermute(values, "fsdp", [((i + step) % size, i) for i in range(size)])


def swap_tensor(values, mask, size):
    return lax.ppermute(values, "tensor", [(i, i ^ mask) for i in range(size)])


def shift_order(size):
    order = []
    for step in range(1, size // 2 + 1):
        order.append(step)
        if size - step != step:
            order.append(size - step)
    return order


def gather_group(shard, sizes, own):
    fsdp_size, context_size = sizes
    own_fsdp, own_context = own
    rows = shard.shape[0]
    pieces = [(0, 0, shard)]
    for far in range(1, fsdp_size):
        pieces.append((far, 0, from_fsdp(shard, far, fsdp_size)))
    for step in shift_order(context_size):
        arrived = from_context(shard, step, context_size)
        pieces.append((0, step, arrived))
        for far in range(1, fsdp_size):
            pieces.append((far, step, from_fsdp(arrived, far, fsdp_size)))
    result = jnp.zeros((fsdp_size * context_size,) + shard.shape, shard.dtype)
    for far, step, piece in pieces:
        index = lax.rem(own_fsdp + far, fsdp_size) * context_size + lax.rem(
            own_context + step, context_size
        )
        result = lax.dynamic_update_index_in_dim(result, piece, index, 0)
    return result.reshape((fsdp_size * context_size * rows,) + shard.shape[1:])


def reduce_group(parts, sizes, own):
    fsdp_size, context_size = sizes
    own_fsdp, own_context = own
    kind = low if parts.shape[1] * parts.shape[2] > 16384 else wide
    parts = parts.reshape((fsdp_size, context_size) + parts.shape[1:])
    total = pick(parts, own_fsdp)
    for step in range(1, fsdp_size):
        piece = pick(parts, lax.rem(own_fsdp + step, fsdp_size)).astype(kind)
        total = total + from_fsdp(piece, fsdp_size - step, fsdp_size).astype(wide)
    result = pick(total, own_context)
    for step in shift_order(context_size):
        piece = pick(total, lax.rem(own_context + step, context_size)).astype(kind)
        result = result + from_context(piece, context_size - step, context_size).astype(wide)
    return result


def pick_columns(values, index, count):
    span = values.shape[1] // count
    result = values[:, :span]
    for place in range(1, count):
        result = jnp.where(index == place, values[:, place * span : (place + 1) * span], result)
    return result


def pick_rows(values, index, count):
    span = values.shape[0] // count
    result = values[:span]
    for place in range(1, count):
        result = jnp.where(index == place, values[place * span : (place + 1) * span], result)
    return result


def pick(values, index):
    return lax.dynamic_index_in_dim(values, index, 0, keepdims=False)


def gather_rows(values, tensor_size):
    blocks = [values]
    mask = tensor_size // 2
    while mask:
        blocks = blocks + [swap_tensor(block, mask, tensor_size) for block in blocks]
        mask //= 2
    return jnp.concatenate(blocks, axis=1)


def mask_order(tensor_size):
    order = [0]
    mask = tensor_size // 2
    while mask:
        order = order + [item ^ mask for item in order]
        mask //= 2
    return order


def scatter_rows(parts, tensor_size, first=1):
    mask = first
    while mask < tensor_size:
        parts = scatter_step(parts, mask, tensor_size)
        mask *= 2
    return parts


def scatter_step(parts, mask, tensor_size):
    half = parts.shape[1] // 2
    arrived = swap_tensor(parts[:, half:].astype(low), mask, tensor_size)
    return parts[:, :half] + arrived.astype(wide)


def norm_stats(values):
    centre = jnp.mean(values, axis=-1, keepdims=True)
    centred = values - centre
    spread = jnp.mean(centred * centred, axis=-1, keepdims=True)
    root = lax.rsqrt(spread + 1e-05)
    return centred * root, root


def layer_norm(values, gain, shift):
    scaled, unused = norm_stats(values)
    return (scaled * gain + shift).astype(low)


def norm_back(values, gain, grad):
    scaled, root = norm_stats(values)
    weighted = grad * gain
    inner = jnp.mean(weighted * scaled, axis=-1, keepdims=True)
    outer = jnp.mean(weighted, axis=-1, keepdims=True)
    piece = root * (weighted - outer - scaled * inner)
    return piece, jnp.sum(grad * scaled, axis=(0, 1)), jnp.sum(grad, axis=(0, 1))


def frame_places(shape, axis, frames, order, own):
    row = lax.broadcasted_iota(jnp.int32, shape, axis)
    place = jnp.zeros(shape, jnp.int32)
    for slot, mask in enumerate(order):
        inside = (row >= slot * frames) & (row < (slot + 1) * frames)
        place = jnp.where(inside, (own ^ mask) * frames + row - slot * frames, place)
    return place


def fill_bias(bias_ref, frames, order, own):
    shape = bias_ref.shape
    keys = frame_places(shape, 0, frames, order, own)
    queries = frame_places(shape, 1, frames, order, own)
    bias_ref[...] = jnp.where(keys <= queries, 0.0, masked_score).astype(wide)


def self_forward_kernel(frames, order, place_ref, rows_ref, out_ref, top_ref, bias_ref):
    blocks, block_rows = rows_ref.shape[0], rows_ref.shape[1]
    width = out_ref.shape[2]
    heads = width // HEAD
    own_block = place_ref[0]
    fill_bias(bias_ref, frames, order, place_ref[1])

    def slot_of(block):
        return lax.rem(own_block - block + blocks, blocks)

    def query_block(block, unused):
        slot = slot_of(block)
        outs = []
        for head in range(heads):
            lanes = head * HEAD
            query = rows_ref[slot, :, lanes : lanes + HEAD] * scale

            def key_value(where, lanes=lanes):
                key = rows_ref[where, :, width + lanes : width + lanes + HEAD]
                value = rows_ref[where, :, 2 * width + lanes : 2 * width + lanes + HEAD]
                return key, value

            key, value = key_value(slot)
            scores = dot(key, query, 1, 1) + bias_ref[...]
            top = jnp.max(scores, axis=0, keepdims=True)
            weights = jnp.exp(scores - top)
            total = jnp.sum(weights, axis=0, keepdims=True)
            acc = dot(value, weights.astype(low), 0, 0)

            def step(past, carry, query=query, key_value=key_value):
                top, total, acc = carry
                key, value = key_value(slot_of(past))
                scores = dot(key, query, 1, 1)
                new_top = jnp.maximum(top, jnp.max(scores, axis=0, keepdims=True))
                weights = jnp.exp(scores - new_top)
                shrink = jnp.exp(top - new_top)
                total = total * shrink + jnp.sum(weights, axis=0, keepdims=True)
                acc = acc * shrink + dot(value, weights.astype(low), 0, 0)
                return new_top, total, acc

            top, total, acc = lax.fori_loop(0, block, step, (top, total, acc))
            outs.append((acc / total).T)
            top_ref[slot, head : head + 1, :] = top + jnp.log(total)
        out_ref[slot] = jnp.concatenate(outs, axis=1).astype(low)
        return unused

    lax.fori_loop(0, blocks, query_block, 0)


def self_backward_kernel(
    frames,
    order,
    place_ref,
    rows_ref,
    out_ref,
    top_ref,
    grad_ref,
    result_ref,
    bias_ref,
    delta_ref,
    query_acc,
    key_acc,
    value_acc,
):
    blocks, block_rows = rows_ref.shape[0], rows_ref.shape[1]
    width = out_ref.shape[2]
    heads = width // HEAD
    own_block = place_ref[0]
    fill_bias(bias_ref, frames, order, place_ref[1])
    query_acc[...] = jnp.zeros_like(query_acc)

    def slot_of(block):
        return lax.rem(own_block - block + blocks, blocks)

    def fill_delta(slot, unused):
        for head in range(heads):
            lanes = head * HEAD
            product = out_ref[slot, :, lanes : lanes + HEAD].astype(wide) * grad_ref[
                slot, :, lanes : lanes + HEAD
            ].astype(wide)
            delta_ref[slot, head : head + 1, :] = jnp.sum(product.T, axis=0, keepdims=True)
        return unused

    lax.fori_loop(0, blocks, fill_delta, 0)

    def key_block(block, unused):
        slot = slot_of(block)
        for head in range(heads):
            lanes = head * HEAD
            key = rows_ref[slot, :, width + lanes : width + lanes + HEAD]
            value = rows_ref[slot, :, 2 * width + lanes : 2 * width + lanes + HEAD]

            def terms(where, bias, lanes=lanes, head=head, key=key, value=value):
                query = rows_ref[where, :, lanes : lanes + HEAD] * scale
                grad = grad_ref[where, :, lanes : lanes + HEAD]
                scores = dot(key, query, 1, 1)
                if bias is not None:
                    scores = scores + bias
                weights = jnp.exp(scores - top_ref[where, head : head + 1, :])
                grad_weights = dot(value, grad, 1, 1)
                grad_scores = (weights * (grad_weights - delta_ref[where, head : head + 1, :])).astype(low)
                query_acc[head, where] += dot(key, grad_scores, 0, 0)
                return dot(grad_scores, query, 1, 0), dot(weights.astype(low), grad, 1, 0)

            start = terms(slot, bias_ref[...])

            def step(later, carry, terms=terms):
                key_part, value_part = terms(slot_of(later), None)
                return carry[0] + key_part, carry[1] + value_part

            key_grad, value_grad = lax.fori_loop(block + 1, blocks, step, start)
            key_acc[head, slot] = key_grad
            value_acc[head, slot] = value_grad
        return unused

    lax.fori_loop(0, blocks, key_block, 0)

    def write(slot, unused):
        parts = [(query_acc[head, slot] * scale).T for head in range(heads)]
        parts += [key_acc[head, slot] for head in range(heads)]
        parts += [value_acc[head, slot] for head in range(heads)]
        rest = result_ref.shape[2] - 3 * width
        if rest:
            parts.append(jnp.zeros((block_rows, rest), wide))
        result_ref[slot] = jnp.concatenate(parts, axis=1).astype(low)
        return unused

    lax.fori_loop(0, blocks, write, 0)


smem = pl.BlockSpec(memory_space=pltpu.SMEM)
vmem = pl.BlockSpec(memory_space=pltpu.VMEM)
kernel_params = pltpu.CompilerParams(vmem_limit_bytes=40 * 1024 * 1024)


def self_forward(place, rows, width, frames, order):
    blocks, block_rows, unused = rows.shape
    heads = width // HEAD
    work = blocks * block_rows * blocks * block_rows * heads * 5 // 8
    return pl.pallas_call(
        functools.partial(self_forward_kernel, frames, order),
        out_shape=(
            jax.ShapeDtypeStruct((blocks, block_rows, width), low),
            jax.ShapeDtypeStruct((blocks, heads, block_rows), wide),
        ),
        in_specs=[smem, vmem],
        out_specs=(vmem, vmem),
        scratch_shapes=[pltpu.VMEM((block_rows, block_rows), wide)],
        compiler_params=kernel_params,
        cost_estimate=pl.CostEstimate(
            flops=work * 64 * 4, bytes_accessed=rows.size * 4, transcendentals=work
        ),
    )(place, rows)


def self_backward(place, rows, out, top, grad, frames, order):
    blocks, block_rows, full = rows.shape
    width = out.shape[2]
    heads = width // HEAD
    work = blocks * block_rows * blocks * block_rows * heads * 5 // 8
    return pl.pallas_call(
        functools.partial(self_backward_kernel, frames, order),
        out_shape=jax.ShapeDtypeStruct((blocks, block_rows, full), low),
        in_specs=[smem, vmem, vmem, vmem, vmem],
        out_specs=vmem,
        scratch_shapes=[
            pltpu.VMEM((block_rows, block_rows), wide),
            pltpu.VMEM((blocks, heads, block_rows), wide),
            pltpu.VMEM((heads, blocks, HEAD, block_rows), wide),
            pltpu.VMEM((heads, blocks, block_rows, HEAD), wide),
            pltpu.VMEM((heads, blocks, block_rows, HEAD), wide),
        ],
        compiler_params=kernel_params,
        cost_estimate=pl.CostEstimate(
            flops=work * 64 * 10, bytes_accessed=rows.size * 8, transcendentals=work
        ),
    )(place, rows, out, top, grad)


def cross_weights(query, key):
    scores = dot(key, query * scale, 1, 1)
    top = jnp.max(scores, axis=0, keepdims=True)
    weights = jnp.exp(scores - top)
    return weights / jnp.sum(weights, axis=0, keepdims=True)


def cross_forward_kernel(query_ref, key_ref, value_ref, out_ref):
    outs = []
    for head in range(query_ref.shape[2] // HEAD):
        lanes = slice(head * HEAD, (head + 1) * HEAD)
        weights = cross_weights(query_ref[0, :, lanes], key_ref[0, :, lanes])
        outs.append(dot(value_ref[0, :, lanes], weights.astype(low), 0, 0).T)
    out_ref[0] = jnp.concatenate(outs, axis=1).astype(low)


def cross_backward_kernel(query_ref, key_ref, value_ref, grad_ref, query_out, key_out, value_out):
    queries, keys, values = [], [], []
    for head in range(query_ref.shape[2] // HEAD):
        lanes = slice(head * HEAD, (head + 1) * HEAD)
        query, key, value = query_ref[0, :, lanes], key_ref[0, :, lanes], value_ref[0, :, lanes]
        grad = grad_ref[0, :, lanes]
        weights = cross_weights(query, key)
        grad_weights = dot(value, grad, 1, 1)
        inner = jnp.sum(weights * grad_weights, axis=0, keepdims=True)
        grad_scores = (weights * (grad_weights - inner)).astype(low)
        queries.append((dot(key, grad_scores, 0, 0) * scale).T)
        keys.append(dot(grad_scores, query * scale, 1, 0))
        values.append(dot(weights.astype(low), grad, 1, 0))
    query_out[0] = jnp.concatenate(queries, axis=1).astype(low)
    key_out[0] = jnp.concatenate(keys, axis=1)
    value_out[0] = jnp.concatenate(values, axis=1)


def clip_spec(shape):
    return pl.BlockSpec((1,) + tuple(shape[1:]), lambda clip: (clip, 0, 0))


def cross_forward(query, key, value):
    work = query.shape[0] * query.shape[1] * query.shape[2] * key.shape[1]
    return pl.pallas_call(
        cross_forward_kernel,
        grid=(query.shape[0],),
        out_shape=jax.ShapeDtypeStruct(query.shape, low),
        in_specs=[clip_spec(query.shape), clip_spec(key.shape), clip_spec(value.shape)],
        out_specs=clip_spec(query.shape),
        compiler_params=kernel_params,
        cost_estimate=pl.CostEstimate(
            flops=4 * work, bytes_accessed=4 * query.size, transcendentals=work // 64
        ),
    )(query, key, value)


def cross_backward(query, key, value, grad):
    work = query.shape[0] * query.shape[1] * query.shape[2] * key.shape[1]
    return pl.pallas_call(
        cross_backward_kernel,
        grid=(query.shape[0],),
        out_shape=(
            jax.ShapeDtypeStruct(query.shape, low),
            jax.ShapeDtypeStruct(key.shape, wide),
            jax.ShapeDtypeStruct(value.shape, wide),
        ),
        in_specs=[
            clip_spec(query.shape),
            clip_spec(key.shape),
            clip_spec(value.shape),
            clip_spec(grad.shape),
        ],
        out_specs=(clip_spec(query.shape), clip_spec(key.shape), clip_spec(value.shape)),
        compiler_params=kernel_params,
        cost_estimate=pl.CostEstimate(
            flops=10 * work, bytes_accessed=8 * query.size, transcendentals=work // 64
        ),
    )(query, key, value, grad)


def to_heads(chunks, own, size):
    slots = {0: pick(chunks, own)}
    for step in shift_order(size):
        chunk = pick(chunks, lax.rem(own + step, size))
        slots[step] = from_context(chunk, size - step, size)
    return [slots[step] for step in range(size)]


def to_frames(slots, own, size):
    arrived = {0: slots[0]}
    for step in shift_order(size):
        arrived[step] = from_context(slots[step], step, size)
    return [arrived[step] for step in range(size)]


def by_sender(arrived, own, size):
    stacked = jnp.stack(arrived)
    return jnp.stack([pick(stacked, lax.rem(j - own + size, size)) for j in range(size)])


def on_device(sizes, frames, text_states, cotangent, *parameters):
    nf, nc, nt = sizes
    (
        self_query,
        self_key,
        self_value,
        self_out,
        cross_query,
        cross_key,
        cross_value,
        cross_out,
        feed_in,
        feed_out,
    ) = parameters[:10]
    own_fsdp = lax.axis_index("fsdp")
    own_context = lax.axis_index("context")
    own_tensor = lax.axis_index("tensor")
    frame_count, clips, features = frames.shape
    order = mask_order(nt)
    block = features // (nf * nc)
    columns = self_query.shape[1]
    halves = nc // clips
    width = columns // halves
    padded = 3 * width
    place = jnp.stack([own_context, own_tensor]).astype(jnp.int32)
    group = ((nf, nc), (own_fsdp, own_context))
    both = ("fsdp", "context")

    def row_major(values):
        return with_layout_constraint(values, Layout(major_to_minor=(0, 1)))

    def gather_near(shard):
        return lax.all_gather(shard, "context", axis=0, tiled=True)

    def gather_far(near):
        return [from_fsdp(near, far, nf) for far in range(1, nf)]

    def gather_place(pieces):
        result = jnp.zeros((nf,) + pieces[0].shape, pieces[0].dtype)
        for far, piece in enumerate(pieces):
            result = lax.dynamic_update_index_in_dim(result, piece, lax.rem(own_fsdp + far, nf), 0)
        return result.reshape((nf * pieces[0].shape[0],) + pieces[0].shape[1:])

    def gather_calls(shard):
        return lax.all_gather(shard, both, axis=0, tiled=True)

    vectors = gather_group(jnp.stack(parameters[10:16] + parameters[10:12]), *group)
    vectors = vectors.reshape(nf * nc, -1, block).transpose(1, 0, 2).reshape(-1, features)
    vectors = vectors.astype(wide)
    pieces = []
    for part in range(halves):
        lanes = slice(part * width, (part + 1) * width)
        pieces += [self_query[:, lanes], self_key[:, lanes], self_value[:, lanes]]
    qkv_all = gather_group(jnp.concatenate(pieces, axis=1), *group)
    second_all = gather_calls(jnp.concatenate([cross_query, cross_out], axis=1))
    third_near = gather_near(jnp.concatenate([self_out, cross_key, cross_value], axis=1))
    feed_in_all = gather_calls(feed_in)
    feed_out_all = gather_calls(feed_out)

    def gather_columns(blocks, first, last):
        mask = first
        while mask >= last:
            blocks = blocks + [swap_tensor(part, mask, nt) for part in blocks]
            mask //= 2
        return blocks

    def side_by_side(blocks):
        return [
            jnp.concatenate([part[:, side * columns : (side + 1) * columns] for part in blocks], axis=1)
            for side in range(2)
        ]

    def scatter_columns(parts, mask=1):
        while mask < nt:
            half = parts.shape[-1] // 2
            arrived = swap_tensor(parts[..., half:].astype(low), mask, nt)
            parts = parts[..., :half] + arrived.astype(wide)
            mask *= 2
        return parts

    def outer_value(products, arrived, start, stop, index=None):
        parts = []
        for k, (left, right) in enumerate(products):
            if index is not None:
                left = pick_columns(left, index, nf)
            value = dot(left, right[:, start:stop], 0, 0)
            for piece in arrived:
                span = piece.shape[1] // len(products)
                piece = piece[:, k * span + start : k * span + stop]
                if index is not None:
                    piece = pick_rows(piece, index, nf)
                value = value + piece.astype(wide)
            parts.append(row_major(value))
        return jnp.concatenate(parts, axis=1)

    def outer_swap(products, arrived, mask):
        half = products[0][1].shape[1] // (2 * mask)
        far = outer_value(products, arrived, half, 2 * half).astype(low)
        return arrived + [swap_tensor(far, mask, nt)]


    residual = frames.transpose(1, 0, 2).astype(wide)
    incoming = cotangent.transpose(1, 0, 2)
    text = text_states.transpose(1, 0, 2)

    def after(*values):
        return lax.optimization_barrier(values)

    def grad_products(*products):
        def block_of(index):
            parts = [
                row_major(dot(pick_columns(left, index, nf), right, 0, 0)) for left, right in products
            ]
            return parts[0] if len(parts) == 1 else jnp.concatenate(parts, axis=1)

        far = [block_of(lax.rem(own_fsdp + step, nf)).astype(low) for step in range(1, nf)]
        return [block_of(own_fsdp)] + far

    def exchange(blocks):
        return blocks[:1] + [
            from_fsdp(piece, nf - 1 - step, nf) for step, piece in enumerate(blocks[1:])
        ]

    def grad_start(*products):
        return exchange(grad_products(*products))

    def block_sum(blocks):
        total = blocks[0]
        for piece in blocks[1:]:
            total = total + piece.astype(wide)
        return total

    def grad_scatter(total):
        return lax.psum_scatter(total, "context", scatter_dimension=0, tiled=True)

    def grad_finish(blocks):
        return grad_scatter(block_sum(blocks).astype(low))

    def by_row(values):
        return values.reshape(-1, values.shape[-1])

    def by_clip(values):
        return values.reshape(clips, -1, values.shape[-1])

    def to_chunks(values, lanes):
        parts = [values[..., j * lanes : (j + 1) * lanes] for j in range(halves)]
        return jnp.stack(parts, axis=1).reshape(clips * halves, values.shape[1], lanes)

    def from_chunks(chunks):
        chunks = chunks.reshape((clips, halves) + chunks.shape[1:])
        return jnp.concatenate([chunks[:, j] for j in range(halves)], axis=-1)

    normed_one = by_row(gather_rows(layer_norm(residual, vectors[0], vectors[1]), nt))
    normed_one, second_all = after(normed_one, second_all)
    second_blocks = gather_columns([second_all], nt // 2, 2)
    projected = by_clip(dot(normed_one, qkv_all, 1, 0).astype(low))
    head_rows = to_heads(to_chunks(projected, padded), own_context, nc)
    head_rows[1], third_near = after(head_rows[1], third_near)
    third_far = gather_far(third_near)
    head_rows = jnp.stack(head_rows)
    head_rows, *second_blocks = after(head_rows, *second_blocks)
    head_out, head_top = self_forward(place, head_rows, width, frame_count, order)
    head_out, *moved = after(head_out, *second_blocks, *third_far)
    second_blocks, third_far = moved[: len(second_blocks)], moved[len(second_blocks) :]
    third_all = gather_place([third_near] + third_far)
    self_out_all = third_all[:, :columns]
    cross_key_value = third_all[:, columns:]
    cross_query_all, cross_out_all = side_by_side(gather_columns(second_blocks, 1, 1))
    attended = to_frames(head_out, own_context, nc)
    attended = by_row(from_chunks(by_sender(attended, own_context, nc)))
    text_projected = dot(by_row(text), cross_key_value, 1, 0).astype(low)
    cross_keys, cross_values = [
        by_clip(part) for part in side_by_side(gather_columns([text_projected], nt // 2, 1))
    ]
    attended, cross_keys, cross_values = after(attended, cross_keys, cross_values)
    after_self = residual + scatter_rows(by_clip(dot(attended, self_out_all, 1, 1)), nt)

    normed_two = by_row(layer_norm(after_self, vectors[2], vectors[3]))
    cross_queries = by_clip(dot(normed_two, cross_query_all, 1, 0).astype(low))
    crossed = cross_forward(cross_queries, cross_keys, cross_values)
    after_cross = after_self + by_clip(dot(by_row(crossed), cross_out_all, 1, 1))

    normed_three = by_row(gather_rows(layer_norm(after_cross, vectors[4], vectors[5]), nt))
    hidden = dot(normed_three, feed_in_all, 1, 0)
    gate = 0.5 + 0.5 * lax.erf(hidden * (0.5**0.5))
    active = (hidden * gate).astype(low)
    grad_rows = by_row(gather_rows(incoming, nt))
    feed_out_blocks = grad_products((grad_rows, active))
    grad_rows, *feed_out_blocks = after(grad_rows, *feed_out_blocks)
    feed_out_blocks = exchange(feed_out_blocks)
    grad_active = dot(grad_rows, feed_out_all, 1, 0)
    slope = gate + hidden * jnp.exp(-0.5 * hidden * hidden) * ((2.0 * jnp.pi) ** -0.5)
    grad_hidden = (grad_active * slope).astype(low)
    grad_normed = scatter_rows(by_clip(dot(grad_hidden, feed_in_all, 1, 1)), nt)
    feed_in_blocks = grad_products((normed_three, grad_hidden))
    grad_normed, *feed_in_blocks = after(grad_normed, *feed_in_blocks)
    piece, third_gain, third_shift = norm_back(after_cross, vectors[4], grad_normed)
    grad_after_cross = incoming.astype(wide) + piece

    cross_rows = by_row(grad_after_cross.astype(low))
    grad_crossed = by_clip(dot(cross_rows, cross_out_all, 1, 0).astype(low))
    grad_cross_queries, grad_cross_keys, grad_cross_values = cross_backward(
        cross_queries, cross_keys, cross_values, grad_crossed
    )
    grad_cross_queries, *feed_in_blocks = after(grad_cross_queries, *feed_in_blocks)
    feed_in_blocks = exchange(feed_in_blocks)
    grad_cross_queries = by_row(grad_cross_queries)
    grad_normed = by_clip(dot(grad_cross_queries, cross_query_all, 1, 1))
    piece, second_gain, second_shift = norm_back(after_self, vectors[2], grad_normed)
    grad_after_self = grad_after_cross + piece
    cross_products = ((cross_rows, by_row(crossed)), (normed_two, grad_cross_queries))
    cross_parts = outer_swap(cross_products, [], 1)

    def text_sum(values, mask):
        arrived = lax.ppermute(values.astype(low), "context", [(i, i ^ mask) for i in range(nc)])
        return values + arrived.astype(wide)

    text_grads = scatter_columns(jnp.stack([by_row(grad_cross_keys), by_row(grad_cross_values)]))
    text_grads = jnp.concatenate([text_grads[0], text_grads[1]], axis=1)
    grad_rows = by_row(gather_rows(grad_after_self.astype(low), nt))
    grad_rows, *feed_out_blocks = after(grad_rows, *feed_out_blocks)
    feed_out_grad = grad_finish(feed_out_blocks)
    grad_attended = by_clip(dot(grad_rows, self_out_all, 1, 0).astype(low))
    head_grad = to_heads(to_chunks(grad_attended, width), own_context, nc)
    first_back = head_grad[nc - 1]
    first_back, grad_rows, text_grads, *cross_parts = after(
        first_back, grad_rows, text_grads, *cross_parts
    )
    head_grad[nc - 1] = first_back
    head_grad = jnp.stack(head_grad)
    mask = 2
    while mask < nt:
        cross_parts = outer_swap(cross_products, cross_parts, mask)
        mask *= 2
    self_out_blocks = grad_start((grad_rows, attended))
    head_grad, feed_out_grad, *feed_in_blocks = after(head_grad, feed_out_grad, *feed_in_blocks)
    feed_out_grad = feed_out_grad.astype(wide)
    feed_in_grad = grad_finish(feed_in_blocks)
    head_back = self_backward(place, head_rows, head_out, head_top, head_grad, frame_count, order)
    head_back, text_grads = after(head_back, text_grads)
    head_back = to_frames(head_back, own_context, nc)
    text_mask = 1
    while 2 * text_mask < nc:
        text_grads = text_sum(text_grads, text_mask)
        text_mask *= 2
    head_back[1], *cross_parts = after(head_back[1], *cross_parts)

    def cross_block(index):
        return outer_value(cross_products, cross_parts, 0, columns, index)

    cross_blocks = [cross_block(own_fsdp)] + [
        from_fsdp(cross_block(lax.rem(own_fsdp + step, nf)).astype(low), nf - step, nf)
        for step in range(1, nf)
    ]
    middle_total = [block_sum(cross_blocks).astype(low), block_sum(self_out_blocks).astype(low)]
    middle_total = jnp.concatenate(middle_total, axis=1)
    far = nc // 2
    head_back[far], middle_total, text_grads = after(head_back[far], middle_total, text_grads)
    text_grads = text_sum(text_grads, text_mask)
    middle_grad = grad_scatter(middle_total)

    grad_projected = by_row(from_chunks(by_sender(head_back, own_context, nc)))
    grad_projected, feed_in_grad = after(grad_projected, feed_in_grad)
    feed_in_grad = feed_in_grad.astype(wide)
    own, *qkv_blocks = grad_products((normed_one, grad_projected))
    grad_projected, *qkv_blocks = after(grad_projected, *qkv_blocks)
    qkv_blocks = exchange([own] + qkv_blocks)
    grad_normed = scatter_step(by_clip(dot(grad_projected, qkv_all, 1, 1)), 1, nt)
    grad_normed, middle_grad, text_grads, *qkv_blocks = after(
        grad_normed, middle_grad, text_grads, *qkv_blocks
    )
    qkv_grad = grad_finish(qkv_blocks).astype(wide)
    text_low = text_grads.astype(low)

    def text_block(step):
        place = lax.rem(own_fsdp + step, nf) * nc + own_context
        return dot(pick_columns(by_row(text), place, nf * nc), text_low, 0, 0)

    text_blocks = [text_block(0)] + [
        from_fsdp(text_block(step).astype(low), nf - step, nf) for step in range(1, nf)
    ]
    text_part = dot(text_low, cross_key_value, 1, 1)
    mask = 1
    while mask < nt:
        text_part = text_part + swap_tensor(text_part.astype(low), mask, nt).astype(wide)
        mask *= 2

    grad_normed = scatter_rows(grad_normed, nt, 2)
    grad_normed, active = after(grad_normed, active)

    layer_out = after_cross + scatter_rows(by_clip(dot(active, feed_out_all, 1, 1)), nt)
    layer_out = layer_out.astype(low).transpose(1, 0, 2)
    key_value_grad = block_sum(text_blocks)
    text_grad = by_clip(text_part).transpose(1, 0, 2)
    middle_grad = middle_grad.astype(wide)
    cross_out_grad = middle_grad[:, :columns]
    cross_query_grad = middle_grad[:, columns : 2 * columns]
    self_out_grad = middle_grad[:, 2 * columns :]
    piece, first_gain, first_shift = norm_back(residual, vectors[0], grad_normed)
    frames_grad = (grad_after_self + piece).transpose(1, 0, 2)

    norm_grads = jnp.stack(
        [first_gain, first_shift, second_gain, second_shift, third_gain, third_shift]
    )
    mask = 1
    while mask < nt:
        norm_grads = norm_grads + swap_tensor(norm_grads, mask, nt)
        mask *= 2
    norm_parts = norm_grads.reshape(6, nf * nc, block).transpose(1, 0, 2)
    norm_result = reduce_group(norm_parts, *group)

    qkv_parts = []
    for kind in range(3):
        parts = [
            qkv_grad[:, part * padded + kind * width : part * padded + (kind + 1) * width]
            for part in range(halves)
        ]
        qkv_parts.append(jnp.concatenate(parts, axis=1))
    return (
        layer_out,
        frames_grad,
        text_grad,
        qkv_parts[0],
        qkv_parts[1],
        qkv_parts[2],
        self_out_grad,
        cross_query_grad,
        key_value_grad[:, :columns],
        key_value_grad[:, columns:],
        cross_out_grad,
        feed_in_grad,
        feed_out_grad,
        norm_result[0],
        norm_result[1],
        norm_result[2],
        norm_result[3],
        norm_result[4],
        norm_result[5],
    )


def solution(mesh):
    sizes = (mesh.shape["fsdp"], mesh.shape["context"], mesh.shape["tensor"])
    rows = P(("context", "tensor"), "fsdp", None)
    texts = P(None, "fsdp", None)
    matrix = P(("fsdp", "context"), "tensor")
    vector = P(("fsdp", "context"))
    return jax.shard_map(
        functools.partial(on_device, sizes),
        mesh=mesh,
        in_specs=(rows, texts, rows) + (matrix,) * 10 + (vector,) * 6,
        out_specs=(rows, rows, texts) + (matrix,) * 10 + (vector,) * 6,
        check_vma=False,
    )
```

```python
import functools

import jax
import jax.numpy as jnp
from jax import lax
from jax.experimental import pallas as pl
from jax.experimental.pallas import tpu as pltpu
from jax.experimental.layout import Layout, with_layout_constraint
from jax.sharding import PartitionSpec as P

HEAD = 64
low = jnp.bfloat16
wide = jnp.float32
masked_score = -1e30
scale = HEAD**-0.5


def dot(left, right, left_dim, right_dim):
    return lax.dot_general(
        left, right, (((left_dim,), (right_dim,)), ((), ())), preferred_element_type=wide
    )


def from_context(values, step, size):
    return lax.ppermute(values, "context", [((i + step) % size, i) for i in range(size)])


def from_fsdp(values, step, size):
    return lax.ppermute(values, "fsdp", [((i + step) % size, i) for i in range(size)])


def swap_tensor(values, mask, size):
    return lax.ppermute(values, "tensor", [(i, i ^ mask) for i in range(size)])


def shift_order(size):
    order = []
    for step in range(1, size // 2 + 1):
        order.append(step)
        if size - step != step:
            order.append(size - step)
    return order


def gather_group(shard, sizes, own):
    fsdp_size, context_size = sizes
    own_fsdp, own_context = own
    rows = shard.shape[0]
    pieces = [(0, 0, shard)]
    for far in range(1, fsdp_size):
        pieces.append((far, 0, from_fsdp(shard, far, fsdp_size)))
    for step in shift_order(context_size):
        arrived = from_context(shard, step, context_size)
        pieces.append((0, step, arrived))
        for far in range(1, fsdp_size):
            pieces.append((far, step, from_fsdp(arrived, far, fsdp_size)))
    result = jnp.zeros((fsdp_size * context_size,) + shard.shape, shard.dtype)
    for far, step, piece in pieces:
        index = lax.rem(own_fsdp + far, fsdp_size) * context_size + lax.rem(
            own_context + step, context_size
        )
        result = lax.dynamic_update_index_in_dim(result, piece, index, 0)
    return result.reshape((fsdp_size * context_size * rows,) + shard.shape[1:])


def reduce_group(parts, sizes, own):
    fsdp_size, context_size = sizes
    own_fsdp, own_context = own
    kind = low if parts.shape[1] * parts.shape[2] > 16384 else wide
    parts = parts.reshape((fsdp_size, context_size) + parts.shape[1:])
    total = pick(parts, own_fsdp)
    for step in range(1, fsdp_size):
        piece = pick(parts, lax.rem(own_fsdp + step, fsdp_size)).astype(kind)
        total = total + from_fsdp(piece, fsdp_size - step, fsdp_size).astype(wide)
    result = pick(total, own_context)
    for step in shift_order(context_size):
        piece = pick(total, lax.rem(own_context + step, context_size)).astype(kind)
        result = result + from_context(piece, context_size - step, context_size).astype(wide)
    return result


def pick_columns(values, index, count):
    span = values.shape[1] // count
    result = values[:, :span]
    for place in range(1, count):
        result = jnp.where(index == place, values[:, place * span : (place + 1) * span], result)
    return result


def pick_rows(values, index, count):
    span = values.shape[0] // count
    result = values[:span]
    for place in range(1, count):
        result = jnp.where(index == place, values[place * span : (place + 1) * span], result)
    return result


def pick(values, index):
    return lax.dynamic_index_in_dim(values, index, 0, keepdims=False)


def gather_rows(values, tensor_size):
    blocks = [values]
    mask = tensor_size // 2
    while mask:
        blocks = blocks + [swap_tensor(block, mask, tensor_size) for block in blocks]
        mask //= 2
    return jnp.concatenate(blocks, axis=1)


def mask_order(tensor_size):
    order = [0]
    mask = tensor_size // 2
    while mask:
        order = order + [item ^ mask for item in order]
        mask //= 2
    return order


def scatter_rows(parts, tensor_size, first=1):
    mask = first
    while mask < tensor_size:
        parts = scatter_step(parts, mask, tensor_size)
        mask *= 2
    return parts


def scatter_step(parts, mask, tensor_size):
    half = parts.shape[1] // 2
    arrived = swap_tensor(parts[:, half:].astype(low), mask, tensor_size)
    return parts[:, :half] + arrived.astype(wide)


def norm_stats(values):
    centre = jnp.mean(values, axis=-1, keepdims=True)
    centred = values - centre
    spread = jnp.mean(centred * centred, axis=-1, keepdims=True)
    root = lax.rsqrt(spread + 1e-05)
    return centred * root, root


def layer_norm(values, gain, shift):
    scaled, unused = norm_stats(values)
    return (scaled * gain + shift).astype(low)


def norm_back(values, gain, grad):
    scaled, root = norm_stats(values)
    weighted = grad * gain
    inner = jnp.mean(weighted * scaled, axis=-1, keepdims=True)
    outer = jnp.mean(weighted, axis=-1, keepdims=True)
    piece = root * (weighted - outer - scaled * inner)
    return piece, jnp.sum(grad * scaled, axis=(0, 1)), jnp.sum(grad, axis=(0, 1))


def frame_places(shape, axis, frames, order, own):
    row = lax.broadcasted_iota(jnp.int32, shape, axis)
    place = jnp.zeros(shape, jnp.int32)
    for slot, mask in enumerate(order):
        inside = (row >= slot * frames) & (row < (slot + 1) * frames)
        place = jnp.where(inside, (own ^ mask) * frames + row - slot * frames, place)
    return place


def fill_bias(bias_ref, frames, order, own):
    shape = bias_ref.shape
    keys = frame_places(shape, 0, frames, order, own)
    queries = frame_places(shape, 1, frames, order, own)
    bias_ref[...] = jnp.where(keys <= queries, 0.0, masked_score).astype(wide)


def self_forward_kernel(frames, order, place_ref, rows_ref, out_ref, top_ref, bias_ref):
    blocks, block_rows = rows_ref.shape[0], rows_ref.shape[1]
    width = out_ref.shape[2]
    heads = width // HEAD
    own_block = place_ref[0]
    fill_bias(bias_ref, frames, order, place_ref[1])

    def slot_of(block):
        return lax.rem(own_block - block + blocks, blocks)

    def query_block(block, unused):
        slot = slot_of(block)
        outs = []
        for head in range(heads):
            lanes = head * HEAD
            query = rows_ref[slot, :, lanes : lanes + HEAD] * scale

            def key_value(where, lanes=lanes):
                key = rows_ref[where, :, width + lanes : width + lanes + HEAD]
                value = rows_ref[where, :, 2 * width + lanes : 2 * width + lanes + HEAD]
                return key, value

            key, value = key_value(slot)
            scores = dot(key, query, 1, 1) + bias_ref[...]
            top = jnp.max(scores, axis=0, keepdims=True)
            weights = jnp.exp(scores - top)
            total = jnp.sum(weights, axis=0, keepdims=True)
            acc = dot(value, weights.astype(low), 0, 0)

            def step(past, carry, query=query, key_value=key_value):
                top, total, acc = carry
                key, value = key_value(slot_of(past))
                scores = dot(key, query, 1, 1)
                new_top = jnp.maximum(top, jnp.max(scores, axis=0, keepdims=True))
                weights = jnp.exp(scores - new_top)
                shrink = jnp.exp(top - new_top)
                total = total * shrink + jnp.sum(weights, axis=0, keepdims=True)
                acc = acc * shrink + dot(value, weights.astype(low), 0, 0)
                return new_top, total, acc

            top, total, acc = lax.fori_loop(0, block, step, (top, total, acc))
            outs.append((acc / total).T)
            top_ref[slot, head : head + 1, :] = top + jnp.log(total)
        out_ref[slot] = jnp.concatenate(outs, axis=1).astype(low)
        return unused

    lax.fori_loop(0, blocks, query_block, 0)


def self_backward_kernel(
    frames,
    order,
    place_ref,
    rows_ref,
    out_ref,
    top_ref,
    grad_ref,
    result_ref,
    bias_ref,
    delta_ref,
    query_acc,
    key_acc,
    value_acc,
):
    blocks, block_rows = rows_ref.shape[0], rows_ref.shape[1]
    width = out_ref.shape[2]
    heads = width // HEAD
    own_block = place_ref[0]
    fill_bias(bias_ref, frames, order, place_ref[1])
    query_acc[...] = jnp.zeros_like(query_acc)

    def slot_of(block):
        return lax.rem(own_block - block + blocks, blocks)

    def fill_delta(slot, unused):
        for head in range(heads):
            lanes = head * HEAD
            product = out_ref[slot, :, lanes : lanes + HEAD].astype(wide) * grad_ref[
                slot, :, lanes : lanes + HEAD
            ].astype(wide)
            delta_ref[slot, head : head + 1, :] = jnp.sum(product.T, axis=0, keepdims=True)
        return unused

    lax.fori_loop(0, blocks, fill_delta, 0)

    def key_block(block, unused):
        slot = slot_of(block)
        for head in range(heads):
            lanes = head * HEAD
            key = rows_ref[slot, :, width + lanes : width + lanes + HEAD]
            value = rows_ref[slot, :, 2 * width + lanes : 2 * width + lanes + HEAD]

            def terms(where, bias, lanes=lanes, head=head, key=key, value=value):
                query = rows_ref[where, :, lanes : lanes + HEAD] * scale
                grad = grad_ref[where, :, lanes : lanes + HEAD]
                scores = dot(key, query, 1, 1)
                if bias is not None:
                    scores = scores + bias
                weights = jnp.exp(scores - top_ref[where, head : head + 1, :])
                grad_weights = dot(value, grad, 1, 1)
                grad_scores = (weights * (grad_weights - delta_ref[where, head : head + 1, :])).astype(low)
                query_acc[head, where] += dot(key, grad_scores, 0, 0)
                return dot(grad_scores, query, 1, 0), dot(weights.astype(low), grad, 1, 0)

            start = terms(slot, bias_ref[...])

            def step(later, carry, terms=terms):
                key_part, value_part = terms(slot_of(later), None)
                return carry[0] + key_part, carry[1] + value_part

            key_grad, value_grad = lax.fori_loop(block + 1, blocks, step, start)
            key_acc[head, slot] = key_grad
            value_acc[head, slot] = value_grad
        return unused

    lax.fori_loop(0, blocks, key_block, 0)

    def write(slot, unused):
        parts = [(query_acc[head, slot] * scale).T for head in range(heads)]
        parts += [key_acc[head, slot] for head in range(heads)]
        parts += [value_acc[head, slot] for head in range(heads)]
        rest = result_ref.shape[2] - 3 * width
        if rest:
            parts.append(jnp.zeros((block_rows, rest), wide))
        result_ref[slot] = jnp.concatenate(parts, axis=1).astype(low)
        return unused

    lax.fori_loop(0, blocks, write, 0)


smem = pl.BlockSpec(memory_space=pltpu.SMEM)
vmem = pl.BlockSpec(memory_space=pltpu.VMEM)
kernel_params = pltpu.CompilerParams(vmem_limit_bytes=40 * 1024 * 1024)


def self_forward(place, rows, width, frames, order):
    blocks, block_rows, unused = rows.shape
    heads = width // HEAD
    work = blocks * block_rows * blocks * block_rows * heads * 5 // 8
    return pl.pallas_call(
        functools.partial(self_forward_kernel, frames, order),
        out_shape=(
            jax.ShapeDtypeStruct((blocks, block_rows, width), low),
            jax.ShapeDtypeStruct((blocks, heads, block_rows), wide),
        ),
        in_specs=[smem, vmem],
        out_specs=(vmem, vmem),
        scratch_shapes=[pltpu.VMEM((block_rows, block_rows), wide)],
        compiler_params=kernel_params,
        cost_estimate=pl.CostEstimate(
            flops=work * 64 * 4, bytes_accessed=rows.size * 4, transcendentals=work
        ),
    )(place, rows)


def self_backward(place, rows, out, top, grad, frames, order):
    blocks, block_rows, full = rows.shape
    width = out.shape[2]
    heads = width // HEAD
    work = blocks * block_rows * blocks * block_rows * heads * 5 // 8
    return pl.pallas_call(
        functools.partial(self_backward_kernel, frames, order),
        out_shape=jax.ShapeDtypeStruct((blocks, block_rows, full), low),
        in_specs=[smem, vmem, vmem, vmem, vmem],
        out_specs=vmem,
        scratch_shapes=[
            pltpu.VMEM((block_rows, block_rows), wide),
            pltpu.VMEM((blocks, heads, block_rows), wide),
            pltpu.VMEM((heads, blocks, HEAD, block_rows), wide),
            pltpu.VMEM((heads, blocks, block_rows, HEAD), wide),
            pltpu.VMEM((heads, blocks, block_rows, HEAD), wide),
        ],
        compiler_params=kernel_params,
        cost_estimate=pl.CostEstimate(
            flops=work * 64 * 10, bytes_accessed=rows.size * 8, transcendentals=work
        ),
    )(place, rows, out, top, grad)


def cross_weights(query, key):
    scores = dot(key, query * scale, 1, 1)
    top = jnp.max(scores, axis=0, keepdims=True)
    weights = jnp.exp(scores - top)
    return weights / jnp.sum(weights, axis=0, keepdims=True)


def cross_forward_kernel(query_ref, key_ref, value_ref, out_ref):
    outs = []
    for head in range(query_ref.shape[2] // HEAD):
        lanes = slice(head * HEAD, (head + 1) * HEAD)
        weights = cross_weights(query_ref[0, :, lanes], key_ref[0, :, lanes])
        outs.append(dot(value_ref[0, :, lanes], weights.astype(low), 0, 0).T)
    out_ref[0] = jnp.concatenate(outs, axis=1).astype(low)


def cross_backward_kernel(query_ref, key_ref, value_ref, grad_ref, query_out, key_out, value_out):
    queries, keys, values = [], [], []
    for head in range(query_ref.shape[2] // HEAD):
        lanes = slice(head * HEAD, (head + 1) * HEAD)
        query, key, value = query_ref[0, :, lanes], key_ref[0, :, lanes], value_ref[0, :, lanes]
        grad = grad_ref[0, :, lanes]
        weights = cross_weights(query, key)
        grad_weights = dot(value, grad, 1, 1)
        inner = jnp.sum(weights * grad_weights, axis=0, keepdims=True)
        grad_scores = (weights * (grad_weights - inner)).astype(low)
        queries.append((dot(key, grad_scores, 0, 0) * scale).T)
        keys.append(dot(grad_scores, query * scale, 1, 0))
        values.append(dot(weights.astype(low), grad, 1, 0))
    query_out[0] = jnp.concatenate(queries, axis=1).astype(low)
    key_out[0] = jnp.concatenate(keys, axis=1)
    value_out[0] = jnp.concatenate(values, axis=1)


def clip_spec(shape):
    return pl.BlockSpec((1,) + tuple(shape[1:]), lambda clip: (clip, 0, 0))


def cross_forward(query, key, value):
    work = query.shape[0] * query.shape[1] * query.shape[2] * key.shape[1]
    return pl.pallas_call(
        cross_forward_kernel,
        grid=(query.shape[0],),
        out_shape=jax.ShapeDtypeStruct(query.shape, low),
        in_specs=[clip_spec(query.shape), clip_spec(key.shape), clip_spec(value.shape)],
        out_specs=clip_spec(query.shape),
        compiler_params=kernel_params,
        cost_estimate=pl.CostEstimate(
            flops=4 * work, bytes_accessed=4 * query.size, transcendentals=work // 64
        ),
    )(query, key, value)


def cross_backward(query, key, value, grad):
    work = query.shape[0] * query.shape[1] * query.shape[2] * key.shape[1]
    return pl.pallas_call(
        cross_backward_kernel,
        grid=(query.shape[0],),
        out_shape=(
            jax.ShapeDtypeStruct(query.shape, low),
            jax.ShapeDtypeStruct(key.shape, wide),
            jax.ShapeDtypeStruct(value.shape, wide),
        ),
        in_specs=[
            clip_spec(query.shape),
            clip_spec(key.shape),
            clip_spec(value.shape),
            clip_spec(grad.shape),
        ],
        out_specs=(clip_spec(query.shape), clip_spec(key.shape), clip_spec(value.shape)),
        compiler_params=kernel_params,
        cost_estimate=pl.CostEstimate(
            flops=10 * work, bytes_accessed=8 * query.size, transcendentals=work // 64
        ),
    )(query, key, value, grad)


def to_heads(chunks, own, size):
    slots = {0: pick(chunks, own)}
    for step in shift_order(size):
        chunk = pick(chunks, lax.rem(own + step, size))
        slots[step] = from_context(chunk, size - step, size)
    return [slots[step] for step in range(size)]


def to_frames(slots, own, size):
    arrived = {0: slots[0]}
    for step in shift_order(size):
        arrived[step] = from_context(slots[step], step, size)
    return [arrived[step] for step in range(size)]


def by_sender(arrived, own, size):
    stacked = jnp.stack(arrived)
    return jnp.stack([pick(stacked, lax.rem(j - own + size, size)) for j in range(size)])


def on_device(sizes, frames, text_states, cotangent, *parameters):
    nf, nc, nt = sizes
    (
        self_query,
        self_key,
        self_value,
        self_out,
        cross_query,
        cross_key,
        cross_value,
        cross_out,
        feed_in,
        feed_out,
    ) = parameters[:10]
    own_fsdp = lax.axis_index("fsdp")
    own_context = lax.axis_index("context")
    own_tensor = lax.axis_index("tensor")
    frame_count, clips, features = frames.shape
    order = mask_order(nt)
    block = features // (nf * nc)
    columns = self_query.shape[1]
    halves = nc // clips
    width = columns // halves
    padded = 3 * width
    place = jnp.stack([own_context, own_tensor]).astype(jnp.int32)
    group = ((nf, nc), (own_fsdp, own_context))
    both = ("fsdp", "context")

    def row_major(values):
        return with_layout_constraint(values, Layout(major_to_minor=(0, 1)))

    def gather_near(shard):
        return lax.all_gather(shard, "context", axis=0, tiled=True)

    def gather_far(near):
        return [from_fsdp(near, far, nf) for far in range(1, nf)]

    def gather_place(pieces):
        result = jnp.zeros((nf,) + pieces[0].shape, pieces[0].dtype)
        for far, piece in enumerate(pieces):
            result = lax.dynamic_update_index_in_dim(result, piece, lax.rem(own_fsdp + far, nf), 0)
        return result.reshape((nf * pieces[0].shape[0],) + pieces[0].shape[1:])

    def gather_calls(shard):
        return lax.all_gather(shard, both, axis=0, tiled=True)

    vectors = gather_group(jnp.stack(parameters[10:16] + parameters[10:12]), *group)
    vectors = vectors.reshape(nf * nc, -1, block).transpose(1, 0, 2).reshape(-1, features)
    vectors = vectors.astype(wide)
    pieces = []
    for part in range(halves):
        lanes = slice(part * width, (part + 1) * width)
        pieces += [self_query[:, lanes], self_key[:, lanes], self_value[:, lanes]]
    qkv_all = gather_group(jnp.concatenate(pieces, axis=1), *group)
    second_all = gather_calls(jnp.concatenate([cross_query, cross_out], axis=1))
    third_near = gather_near(jnp.concatenate([self_out, cross_key, cross_value], axis=1))
    feed_in_all = gather_calls(feed_in)
    feed_out_all = gather_calls(feed_out)

    def gather_columns(blocks, first, last):
        mask = first
        while mask >= last:
            blocks = blocks + [swap_tensor(part, mask, nt) for part in blocks]
            mask //= 2
        return blocks

    def side_by_side(blocks):
        return [
            jnp.concatenate([part[:, side * columns : (side + 1) * columns] for part in blocks], axis=1)
            for side in range(2)
        ]

    def scatter_columns(parts, mask=1):
        while mask < nt:
            half = parts.shape[-1] // 2
            arrived = swap_tensor(parts[..., half:].astype(low), mask, nt)
            parts = parts[..., :half] + arrived.astype(wide)
            mask *= 2
        return parts

    def outer_value(products, arrived, start, stop, index=None):
        parts = []
        for k, (left, right) in enumerate(products):
            if index is not None:
                left = pick_columns(left, index, nf)
            value = dot(left, right[:, start:stop], 0, 0)
            for piece in arrived:
                span = piece.shape[1] // len(products)
                piece = piece[:, k * span + start : k * span + stop]
                if index is not None:
                    piece = pick_rows(piece, index, nf)
                value = value + piece.astype(wide)
            parts.append(row_major(value))
        return jnp.concatenate(parts, axis=1)

    def outer_swap(products, arrived, mask):
        half = products[0][1].shape[1] // (2 * mask)
        far = outer_value(products, arrived, half, 2 * half).astype(low)
        return arrived + [swap_tensor(far, mask, nt)]


    residual = frames.transpose(1, 0, 2).astype(wide)
    incoming = cotangent.transpose(1, 0, 2)
    text = text_states.transpose(1, 0, 2)

    def after(*values):
        return lax.optimization_barrier(values)

    def grad_products(*products):
        def block_of(index):
            parts = [
                row_major(dot(pick_columns(left, index, nf), right, 0, 0)) for left, right in products
            ]
            return parts[0] if len(parts) == 1 else jnp.concatenate(parts, axis=1)

        far = [block_of(lax.rem(own_fsdp + step, nf)).astype(low) for step in range(1, nf)]
        return [block_of(own_fsdp)] + far

    def exchange(blocks):
        return blocks[:1] + [
            from_fsdp(piece, nf - 1 - step, nf) for step, piece in enumerate(blocks[1:])
        ]

    def grad_start(*products):
        return exchange(grad_products(*products))

    def block_sum(blocks):
        total = blocks[0]
        for piece in blocks[1:]:
            total = total + piece.astype(wide)
        return total

    def grad_scatter(total):
        return lax.psum_scatter(total, "context", scatter_dimension=0, tiled=True)

    def grad_finish(blocks):
        return grad_scatter(block_sum(blocks).astype(low))

    def by_row(values):
        return values.reshape(-1, values.shape[-1])

    def by_clip(values):
        return values.reshape(clips, -1, values.shape[-1])

    def to_chunks(values, lanes):
        parts = [values[..., j * lanes : (j + 1) * lanes] for j in range(halves)]
        return jnp.stack(parts, axis=1).reshape(clips * halves, values.shape[1], lanes)

    def from_chunks(chunks):
        chunks = chunks.reshape((clips, halves) + chunks.shape[1:])
        return jnp.concatenate([chunks[:, j] for j in range(halves)], axis=-1)

    normed_one = by_row(gather_rows(layer_norm(residual, vectors[0], vectors[1]), nt))
    normed_one, second_all = after(normed_one, second_all)
    second_blocks = gather_columns([second_all], nt // 2, 2)
    projected = by_clip(dot(normed_one, qkv_all, 1, 0).astype(low))
    head_rows = to_heads(to_chunks(projected, padded), own_context, nc)
    head_rows[1], third_near = after(head_rows[1], third_near)
    third_far = gather_far(third_near)
    head_rows = jnp.stack(head_rows)
    head_rows, *second_blocks = after(head_rows, *second_blocks)
    head_out, head_top = self_forward(place, head_rows, width, frame_count, order)
    head_out, *moved = after(head_out, *second_blocks, *third_far)
    second_blocks, third_far = moved[: len(second_blocks)], moved[len(second_blocks) :]
    third_all = gather_place([third_near] + third_far)
    self_out_all = third_all[:, :columns]
    cross_key_value = third_all[:, columns:]
    cross_query_all, cross_out_all = side_by_side(gather_columns(second_blocks, 1, 1))
    attended = to_frames(head_out, own_context, nc)
    attended = by_row(from_chunks(by_sender(attended, own_context, nc)))
    text_projected = dot(by_row(text), cross_key_value, 1, 0).astype(low)
    cross_keys, cross_values = [
        by_clip(part) for part in side_by_side(gather_columns([text_projected], nt // 2, 1))
    ]
    attended, cross_keys, cross_values = after(attended, cross_keys, cross_values)
    after_self = residual + scatter_rows(by_clip(dot(attended, self_out_all, 1, 1)), nt)

    normed_two = by_row(layer_norm(after_self, vectors[2], vectors[3]))
    cross_queries = by_clip(dot(normed_two, cross_query_all, 1, 0).astype(low))
    crossed = cross_forward(cross_queries, cross_keys, cross_values)
    after_cross = after_self + by_clip(dot(by_row(crossed), cross_out_all, 1, 1))

    normed_three = by_row(gather_rows(layer_norm(after_cross, vectors[4], vectors[5]), nt))
    hidden = dot(normed_three, feed_in_all, 1, 0)
    gate = 0.5 + 0.5 * lax.erf(hidden * (0.5**0.5))
    active = (hidden * gate).astype(low)
    grad_rows = by_row(gather_rows(incoming, nt))
    feed_out_blocks = grad_products((grad_rows, active))
    grad_rows, *feed_out_blocks = after(grad_rows, *feed_out_blocks)
    feed_out_blocks = exchange(feed_out_blocks)
    grad_active = dot(grad_rows, feed_out_all, 1, 0)
    slope = gate + hidden * jnp.exp(-0.5 * hidden * hidden) * ((2.0 * jnp.pi) ** -0.5)
    grad_hidden = (grad_active * slope).astype(low)
    grad_normed = scatter_rows(by_clip(dot(grad_hidden, feed_in_all, 1, 1)), nt)
    feed_in_blocks = grad_products((normed_three, grad_hidden))
    grad_normed, *feed_in_blocks = after(grad_normed, *feed_in_blocks)
    piece, third_gain, third_shift = norm_back(after_cross, vectors[4], grad_normed)
    grad_after_cross = incoming.astype(wide) + piece

    cross_rows = by_row(grad_after_cross.astype(low))
    grad_crossed = by_clip(dot(cross_rows, cross_out_all, 1, 0).astype(low))
    grad_cross_queries, grad_cross_keys, grad_cross_values = cross_backward(
        cross_queries, cross_keys, cross_values, grad_crossed
    )
    grad_cross_queries, *feed_in_blocks = after(grad_cross_queries, *feed_in_blocks)
    feed_in_blocks = exchange(feed_in_blocks)
    grad_cross_queries = by_row(grad_cross_queries)
    grad_normed = by_clip(dot(grad_cross_queries, cross_query_all, 1, 1))
    piece, second_gain, second_shift = norm_back(after_self, vectors[2], grad_normed)
    grad_after_self = grad_after_cross + piece
    cross_products = ((cross_rows, by_row(crossed)), (normed_two, grad_cross_queries))
    cross_parts = outer_swap(cross_products, [], 1)

    def text_sum(values, mask):
        arrived = lax.ppermute(values.astype(low), "context", [(i, i ^ mask) for i in range(nc)])
        return values + arrived.astype(wide)

    text_grads = scatter_columns(jnp.stack([by_row(grad_cross_keys), by_row(grad_cross_values)]))
    text_grads = jnp.concatenate([text_grads[0], text_grads[1]], axis=1)
    grad_rows = by_row(gather_rows(grad_after_self.astype(low), nt))
    grad_rows, *feed_out_blocks = after(grad_rows, *feed_out_blocks)
    feed_out_grad = grad_finish(feed_out_blocks)
    grad_attended = by_clip(dot(grad_rows, self_out_all, 1, 0).astype(low))
    head_grad = to_heads(to_chunks(grad_attended, width), own_context, nc)
    first_back = head_grad[nc - 1]
    first_back, grad_rows, text_grads, *cross_parts = after(
        first_back, grad_rows, text_grads, *cross_parts
    )
    head_grad[nc - 1] = first_back
    head_grad = jnp.stack(head_grad)
    mask = 2
    while mask < nt:
        cross_parts = outer_swap(cross_products, cross_parts, mask)
        mask *= 2
    self_out_blocks = grad_start((grad_rows, attended))
    head_grad, feed_out_grad, *feed_in_blocks = after(head_grad, feed_out_grad, *feed_in_blocks)
    feed_out_grad = feed_out_grad.astype(wide)
    feed_in_grad = grad_finish(feed_in_blocks)
    head_back = self_backward(place, head_rows, head_out, head_top, head_grad, frame_count, order)
    head_back, text_grads = after(head_back, text_grads)
    head_back = to_frames(head_back, own_context, nc)
    text_mask = 1
    while 2 * text_mask < nc:
        text_grads = text_sum(text_grads, text_mask)
        text_mask *= 2
    head_back[1], *cross_parts = after(head_back[1], *cross_parts)

    def cross_block(index):
        return outer_value(cross_products, cross_parts, 0, columns, index)

    cross_blocks = [cross_block(own_fsdp)] + [
        from_fsdp(cross_block(lax.rem(own_fsdp + step, nf)).astype(low), nf - step, nf)
        for step in range(1, nf)
    ]
    middle_total = [block_sum(cross_blocks).astype(low), block_sum(self_out_blocks).astype(low)]
    middle_total = jnp.concatenate(middle_total, axis=1)
    far = nc // 2
    head_back[far], middle_total, text_grads = after(head_back[far], middle_total, text_grads)
    text_grads = text_sum(text_grads, text_mask)
    middle_grad = grad_scatter(middle_total)

    grad_projected = by_row(from_chunks(by_sender(head_back, own_context, nc)))
    grad_projected, feed_in_grad = after(grad_projected, feed_in_grad)
    feed_in_grad = feed_in_grad.astype(wide)
    own, *qkv_blocks = grad_products((normed_one, grad_projected))
    grad_projected, *qkv_blocks = after(grad_projected, *qkv_blocks)
    qkv_blocks = exchange([own] + qkv_blocks)
    grad_normed = scatter_step(by_clip(dot(grad_projected, qkv_all, 1, 1)), 1, nt)
    grad_normed = scatter_rows(grad_normed, nt, 2)
    grad_normed, middle_grad, text_grads, *qkv_blocks = after(
        grad_normed, middle_grad, text_grads, *qkv_blocks
    )
    qkv_total = block_sum(qkv_blocks).astype(low)
    qkv_total, grad_normed, text_grads, active = after(qkv_total, grad_normed, text_grads, active)
    qkv_grad = grad_scatter(qkv_total)
    text_low = text_grads.astype(low)

    def text_block(step):
        place = lax.rem(own_fsdp + step, nf) * nc + own_context
        return dot(pick_columns(by_row(text), place, nf * nc), text_low, 0, 0)

    text_blocks = [text_block(0)] + [
        from_fsdp(text_block(step).astype(low), nf - step, nf) for step in range(1, nf)
    ]
    text_part = dot(text_low, cross_key_value, 1, 1)
    mask = 1
    while mask < nt:
        text_part = text_part + swap_tensor(text_part.astype(low), mask, nt).astype(wide)
        mask *= 2


    layer_out = after_cross + scatter_rows(by_clip(dot(active, feed_out_all, 1, 1)), nt)
    layer_out = layer_out.astype(low).transpose(1, 0, 2)
    key_value_grad = block_sum(text_blocks)
    text_grad = by_clip(text_part).transpose(1, 0, 2)
    middle_grad = middle_grad.astype(wide)
    cross_out_grad = middle_grad[:, :columns]
    cross_query_grad = middle_grad[:, columns : 2 * columns]
    self_out_grad = middle_grad[:, 2 * columns :]
    piece, first_gain, first_shift = norm_back(residual, vectors[0], grad_normed)
    frames_grad = (grad_after_self + piece).transpose(1, 0, 2)

    norm_grads = jnp.stack(
        [first_gain, first_shift, second_gain, second_shift, third_gain, third_shift]
    )
    mask = 1
    while mask < nt:
        norm_grads = norm_grads + swap_tensor(norm_grads, mask, nt)
        mask *= 2
    norm_grads, qkv_grad, layer_out = after(norm_grads, qkv_grad, layer_out)
    qkv_grad = qkv_grad.astype(wide)
    norm_parts = norm_grads.reshape(6, nf * nc, block).transpose(1, 0, 2)
    norm_result = reduce_group(norm_parts, *group)

    qkv_parts = []
    for kind in range(3):
        parts = [
            qkv_grad[:, part * padded + kind * width : part * padded + (kind + 1) * width]
            for part in range(halves)
        ]
        qkv_parts.append(jnp.concatenate(parts, axis=1))
    return (
        layer_out,
        frames_grad,
        text_grad,
        qkv_parts[0],
        qkv_parts[1],
        qkv_parts[2],
        self_out_grad,
        cross_query_grad,
        key_value_grad[:, :columns],
        key_value_grad[:, columns:],
        cross_out_grad,
        feed_in_grad,
        feed_out_grad,
        norm_result[0],
        norm_result[1],
        norm_result[2],
        norm_result[3],
        norm_result[4],
        norm_result[5],
    )


def solution(mesh):
    sizes = (mesh.shape["fsdp"], mesh.shape["context"], mesh.shape["tensor"])
    rows = P(("context", "tensor"), "fsdp", None)
    texts = P(None, "fsdp", None)
    matrix = P(("fsdp", "context"), "tensor")
    vector = P(("fsdp", "context"))
    return jax.shard_map(
        functools.partial(on_device, sizes),
        mesh=mesh,
        in_specs=(rows, texts, rows) + (matrix,) * 10 + (vector,) * 6,
        out_specs=(rows, rows, texts) + (matrix,) * 10 + (vector,) * 6,
        check_vma=False,
    )
```
